32 devices in a mesh: tm: 2 (over x), space: 16 (over z, y, core).
Axes of the slice: x: 2, y: 2, z: 4, core: 2. Of those that a mesh axis runs over, the one named last changes fastest.
Arguments:
- start_state: float32 [2, 2, 1024, 1024], P('tm', None, 'space'), may hold values from -6 to 6
- rigidity: float32 [1024, 1024], P('space'), may hold values from 0.5 to 2
- inv_mass: float32 [1024, 1024], P('space'), may hold values from 0.5 to 2
- gust_load: float32 [1024, 1024], P('space'), may hold values from -6 to 6
- kl_coeff: float32 [4, 4], replicated, may hold values from -3 to 3
- gust_history: float32 [8], P('tm'), may hold values from -4 to 4
Outputs:
- end_state: float32 [2, 2, 1024, 1024], P('tm', None, 'space')
The draws below stay inside these ranges and needn't reach their ends.
All inputs are finite; a program needn't handle non-finite values.
Results may differ from the reference program's by a relative error of at most 0.000082.
Values sent between devices are 32-bit elements; how exact they have to be, the bound alone decides.
No kernel may reach another device: no remote copies, remote signals or barrier semaphores. Data moves between devices by JAX's collectives and lax.ppermute only.
A program may use at most 64 MiB of HBM per device.

```python
import math
import jax
import jax.numpy as jnp
from jax import lax

NY = 1024
FINE = 4
ITERS = 2
KL = 4
SLICES = 2
NX = 1024
STEPS = 8


def block_levels(own_key, shape, shards, low, top_value):
    def one(dim, shards_of):
        steps = jax.random.uniform(jax.random.fold_in(jax.random.fold_in(own_key, 6), dim), (shards_of,), jnp.float32, low / len(shards), top_value / len(shards))
        return jnp.repeat(jnp.exp(steps), shape[dim] // shards_of).reshape((-1,) + (1,) * (len(shape) - dim - 1))

    factor_of = one(*shards[0])
    for cut in shards[1:]:
        factor_of = factor_of * one(*cut)
    return factor_of


def scatter_about(own_key, dims, deviation, limit, shards=(), dtype=jnp.bfloat16):
    factor_of = block_levels(own_key, dims, shards, -0.22, 0.18) if shards else 1.0
    values = jax.random.normal(own_key, dims, jnp.float32) * deviation * factor_of
    return jnp.minimum(jnp.maximum(values, -limit), limit).astype(dtype)


def setup_inputs(seed: int = 0) -> dict:
    key_list = jax.random.split(jax.random.key(seed), 7)
    return {
        "start_state": scatter_about(key_list[0], (SLICES, 2, NX, NY), 1.0, 6.0, ((0, 2), (2, 16)), jnp.float32),
        "rigidity": jnp.clip(jnp.exp(math.log(2.0) - 1.3862944 * jax.random.uniform(key_list[1], (NX, NY), jnp.float32) ** block_levels(key_list[1], (NX, NY), ((0, 16),), -0.2, 0.2)), 0.5, 2.0),
        "inv_mass": jnp.clip(jnp.exp(math.log(2.0) - 1.3862944 * jax.random.uniform(key_list[2], (NX, NY), jnp.float32) ** block_levels(key_list[2], (NX, NY), ((0, 16),), -0.2, 0.2)), 0.5, 2.0),
        "gust_load": scatter_about(key_list[3], (NX, NY), 1.0, 6.0, ((0, 16),), jnp.float32),
        "kl_coeff": scatter_about(key_list[4], (KL, KL), 1.0, 3.0, (), jnp.float32),
        "gust_history": scatter_about(key_list[5], (STEPS,), 1.0, 4.0, ((0, 2),), jnp.float32),
    }


STIFF_SCALE = 1.0 / 64.0
TIME_STEP = 0.18
HALF_STEP = 0.09
DAMPING = 0.05


def laplace(padded):
    return padded[2:, 1:-1] + padded[:-2, 1:-1] + padded[1:-1, 2:] + padded[1:-1, :-2] - 4.0 * padded[1:-1, 1:-1]


def mode_table(positions, extent):
    orders = (jnp.arange(KL) + 1).astype(jnp.float32)
    coords = (positions.astype(jnp.float32) + 0.5) / extent
    return jnp.cos(jnp.pi * orders[:, None] * coords[None, :])


def build_rigidity(rigidity, kl_coeff, first_row, extent_rows, extent_cols):
    row_count = rigidity.shape[0]
    col_count = rigidity.shape[1]
    across = mode_table(first_row + jnp.arange(row_count).astype(jnp.int32), extent_rows)
    along_chord = mode_table(jnp.arange(col_count).astype(jnp.int32), extent_cols)
    mixed = jnp.dot(kl_coeff, along_chord, precision=lax.Precision.HIGHEST)
    kl_field = jnp.dot(across.T, mixed, precision=lax.Precision.HIGHEST)
    return rigidity * jnp.exp(0.5 * jnp.tanh(kl_field))


def stiffness(position, stiff_field):
    weighted = stiff_field * laplace(jnp.pad(position, 1))
    return STIFF_SCALE * laplace(jnp.pad(weighted, 1))


def accelerate(position, velocity, stiff_now, inv_mass, gust_load, gust_value):
    return inv_mass * (gust_load * gust_value - stiff_now) - DAMPING * velocity


def coarse_step(position, velocity, stiff_now, inv_mass, gust_load, gust_value):
    coarse_span = FINE * TIME_STEP
    new_vel = velocity + coarse_span * accelerate(position, velocity, stiff_now, inv_mass, gust_load, gust_value)
    return position + coarse_span * new_vel, new_vel


def fine_run(position, velocity, stiff_field, inv_mass, gust_load, gust_values):
    stiff_now = stiffness(position, stiff_field)
    first_stiff = stiff_now
    for step_index in range(FINE):
        gust_value = gust_values[step_index]
        half_vel = velocity + HALF_STEP * accelerate(position, velocity, stiff_now, inv_mass, gust_load, gust_value)
        position = position + TIME_STEP * half_vel
        stiff_now = stiffness(position, stiff_field)
        velocity = half_vel + HALF_STEP * accelerate(position, half_vel, stiff_now, inv_mass, gust_load, gust_value)
    return position, velocity, first_stiff


def reference(start_state, rigidity, inv_mass, gust_load, kl_coeff, gust_history):
    stiff_field = build_rigidity(rigidity, kl_coeff, 0, NX, NY)
    starts = [(start_state[slice_index, 0], start_state[slice_index, 1]) for slice_index in range(SLICES)]
    end_states = []
    for sweep_index in range(ITERS):
        deltas = []
        for slice_index in range(SLICES):
            values = gust_history[slice_index * FINE:(slice_index + 1) * FINE]
            base_pos, base_vel = starts[slice_index]
            fine_pos, fine_vel, first_stiff = fine_run(base_pos, base_vel, stiff_field, inv_mass, gust_load, values)
            coarse_pos, coarse_vel = coarse_step(base_pos, base_vel, first_stiff, inv_mass, gust_load, values[0])
            deltas.append((fine_pos - coarse_pos, fine_vel - coarse_vel))
        chain_pos, chain_vel = starts[0]
        end_states = []
        for slice_index in range(SLICES):
            stiff_now = stiffness(chain_pos, stiff_field)
            moved_pos, moved_vel = coarse_step(chain_pos, chain_vel, stiff_now, inv_mass, gust_load, gust_history[slice_index * FINE])
            chain_pos = moved_pos + deltas[slice_index][0]
            chain_vel = moved_vel + deltas[slice_index][1]
            end_states.append(jnp.stack([chain_pos, chain_vel]))
        starts = [starts[0]] + [(end_states[slice_index][0], end_states[slice_index][1]) for slice_index in range(SLICES - 1)]
    return jnp.stack(end_states)
```

```python
import functools

import jax
import jax.numpy as jnp
from jax import lax
from jax.experimental import pallas as pl
from jax.experimental.pallas import tpu as pltpu
from jax.sharding import PartitionSpec as P

FINE = 4
ITERS = 2
KL = 4


STIFF_SCALE = 1.0 / 64.0
TIME_STEP = 0.18
HALF_STEP = 0.09
DAMPING = 0.05


def extended(block, sides, width):
    for axis, dim in sides:
        count = lax.axis_size(axis)
        forward = [(i, i + 1) for i in range(count - 1)]
        backward = [(target, source) for source, target in forward]
        low = lax.ppermute(
            lax.slice_in_dim(block, block.shape[dim] - width, None, axis=dim), axis, forward
        )
        high = lax.ppermute(lax.slice_in_dim(block, 0, width, axis=dim), axis, backward)
        block = jnp.concatenate([low, block, high], axis=dim)
    return block


def passed_along(block, axis, distance):
    devices = range(lax.axis_size(axis))
    route = [(i - distance, i) for i in devices if i - distance in devices]
    return lax.ppermute(block, axis, route)


def laplace(padded):
    return (
        padded[2:, 1:-1]
        + padded[:-2, 1:-1]
        + padded[1:-1, 2:]
        + padded[1:-1, :-2]
        - 4.0 * padded[1:-1, 1:-1]
    )


def mode_table(positions, extent):
    orders = (jnp.arange(KL) + 1).astype(jnp.float32)
    coords = (positions.astype(jnp.float32) + 0.5) / extent
    return jnp.cos(jnp.pi * orders[:, None] * coords[None, :])


def build_rigidity(rigidity, kl_coeff, first_row, extent_rows, extent_cols):
    row_count = rigidity.shape[0]
    col_count = rigidity.shape[1]
    across = mode_table(first_row + jnp.arange(row_count), extent_rows)
    along_chord = mode_table(jnp.arange(col_count), extent_cols)
    mixed = jnp.dot(kl_coeff, along_chord, precision=lax.Precision.HIGHEST)
    kl_field = jnp.dot(across.T, mixed, precision=lax.Precision.HIGHEST)
    return rigidity * jnp.exp(0.5 * jnp.tanh(kl_field))


def apply_padded(widened, rigid_rim):
    weighted = rigid_rim * laplace(jnp.pad(widened, ((0, 0), (1, 1))))
    return STIFF_SCALE * laplace(jnp.pad(weighted, ((0, 0), (1, 1))))


def crop_rows(values_in, have_rim, want_rim):
    margin = have_rim - want_rim
    return values_in[margin : values_in.shape[0] - margin]


def accelerate(velocity, stiff_now, inv_mass, gust_load, gust_value):
    return inv_mass * (gust_load * gust_value - stiff_now) - DAMPING * velocity


def coarse_step(position, velocity, stiff_now, inv_mass, gust_load, gust_value):
    coarse_span = FINE * TIME_STEP
    new_vel = velocity + coarse_span * accelerate(
        velocity, stiff_now, inv_mass, gust_load, gust_value
    )
    return (position + coarse_span * new_vel, new_vel)


def per_device(start_state, rigidity, inv_mass, gust_load, kl_coeff, gust_history):
    row_count = rigidity.shape[0]
    col_count = rigidity.shape[1]
    space_count = lax.axis_size("space")
    time_count = lax.axis_size("tm")
    time_slot = lax.axis_index("tm")
    space_slot = lax.axis_index("space")
    stiff_field = build_rigidity(
        rigidity, kl_coeff, space_slot * row_count, row_count * space_count, col_count
    )
    reach = 2 * (FINE + 1)
    statics = extended(jnp.stack([stiff_field, inv_mass, gust_load]), (("space", 1),), reach)
    rigid_wide = statics[0]
    mass_wide = statics[1]
    load_wide = statics[2]
    rigid_one = crop_rows(rigid_wide, reach, 1)

    def coarse_stiff(moved):
        widened = extended(moved, (("space", 0),), 2)
        return apply_padded(widened, rigid_one)

    def coarse_move(position, velocity, stiff_now, gust_value):
        return coarse_step(position, velocity, stiff_now, inv_mass, gust_load, gust_value)

    position = start_state[0, 0]
    velocity = start_state[0, 1]
    end_pos = position
    end_vel = velocity
    for sweep_index in range(ITERS):
        last_sweep = sweep_index == ITERS - 1
        both = extended(jnp.stack([position, velocity]), (("space", 1),), reach)
        rim_now = reach
        fine_stiff_now = apply_padded(both[0], crop_rows(rigid_wide, reach, rim_now - 1))
        next_rim = rim_now - 2
        first_stiff = crop_rows(fine_stiff_now, next_rim, 0)
        pos_now = crop_rows(both[0], rim_now, next_rim)
        vel_now = crop_rows(both[1], rim_now, next_rim)
        rim_now = next_rim
        for step_index in range(FINE):
            fine_gust_value = gust_history[step_index]
            mass_now = crop_rows(mass_wide, reach, rim_now)
            load_now = crop_rows(load_wide, reach, rim_now)
            half_vel = vel_now + HALF_STEP * accelerate(
                vel_now, fine_stiff_now, mass_now, load_now, fine_gust_value
            )
            pos_now = pos_now + TIME_STEP * half_vel
            fine_stiff_now = apply_padded(pos_now, crop_rows(rigid_wide, reach, rim_now - 1))
            next_rim = rim_now - 2
            pos_now = crop_rows(pos_now, rim_now, next_rim)
            half_vel = crop_rows(half_vel, rim_now, next_rim)
            mass_now = crop_rows(mass_wide, reach, next_rim)
            load_now = crop_rows(load_wide, reach, next_rim)
            vel_now = half_vel + HALF_STEP * accelerate(
                half_vel, fine_stiff_now, mass_now, load_now, fine_gust_value
            )
            rim_now = next_rim
        fine_pos, fine_vel, first_stiff = (pos_now, vel_now, first_stiff)
        coarse_pos, coarse_vel = coarse_move(position, velocity, first_stiff, gust_history[0])
        delta_pos = fine_pos - coarse_pos
        delta_vel = fine_vel - coarse_vel
        chain_pos = position
        chain_vel = velocity
        for turn_index in range(1, time_count):
            stiff_now = coarse_stiff(chain_pos)
            moved_pos, moved_vel = coarse_move(chain_pos, chain_vel, stiff_now, gust_history[0])
            outgoing = jnp.stack([moved_pos + delta_pos, moved_vel + delta_vel])
            arrived = passed_along(outgoing, "tm", 1)
            chain_pos = jnp.where(time_slot == turn_index, arrived[0], chain_pos)
            chain_vel = jnp.where(time_slot == turn_index, arrived[1], chain_vel)
        if last_sweep:
            stiff_now = coarse_stiff(chain_pos)
            moved_pos, moved_vel = coarse_move(chain_pos, chain_vel, stiff_now, gust_history[0])
            end_pos = moved_pos + delta_pos
            end_vel = moved_vel + delta_vel
        position = chain_pos
        velocity = chain_vel
    return jnp.stack([end_pos, end_vel])[None]


LANES = 128
SUBLANES = 8
COARSE_SPAN = FINE * TIME_STEP
DECAY = 1.0 - HALF_STEP * DAMPING
COARSE_DECAY = 1.0 - COARSE_SPAN * DAMPING
KICK = TIME_STEP * HALF_STEP
UNROLL = 8


def tile_view(block):
    width = block.shape[-1] // LANES
    tiles = block.reshape(-1, SUBLANES, width, LANES).transpose(0, 2, 1, 3)
    return tiles.reshape(-1, LANES)


def from_tile_view(view, shape):
    width = shape[-1] // LANES
    tiles = view.reshape(-1, width, SUBLANES, LANES).transpose(0, 2, 1, 3)
    return tiles.reshape(shape)


def row_at(view_ref, group, row):
    start = pl.multiple_of(group * SUBLANES * SUBLANES, SUBLANES * SUBLANES)
    return view_ref[pl.ds(start + row, SUBLANES, stride=SUBLANES), :]


def pack_kernel(gust_ref, view_ref, edge_ref, mid_ref, *, rows, far, near):
    sub = lax.broadcasted_iota(jnp.int32, (SUBLANES, LANES), 0)
    gusts = jnp.zeros((SUBLANES, LANES), jnp.float32)
    for step_index in range(FINE):
        gusts = jnp.where(sub == step_index, gust_ref[step_index], gusts)
    side = far + near
    edge_ref[2 * side] = gusts
    for part, width, at in ((0, far, 0), (1, near, far)):
        for row in range(rows):
            group = (part * rows + row) // SUBLANES
            value = row_at(view_ref, group, row % SUBLANES)
            if row < width:
                edge_ref[at + row] = value
            elif row >= rows - width:
                edge_ref[side + at + row - (rows - width)] = value
            else:
                mid_ref[part * (rows - 2 * far) + row - width] = value


def field_kernel(
    kl_ref, across_ref, along_ref, rigid_ref, mass_ref, load_ref, stiff_ref, pull_ref, push_ref
):
    rows = stiff_ref.shape[0]
    mixed = []
    for order in range(KL):
        total = kl_ref[order, 0] * along_ref[0]
        for other in range(1, KL):
            total = total + kl_ref[order, other] * along_ref[other]
        mixed.append(total)

    def group_rows(group, carry):
        for row in range(SUBLANES):
            at = group * SUBLANES + row
            field = across_ref[0, at] * mixed[0]
            for order in range(1, KL):
                field = field + across_ref[order, at] * mixed[order]
            mass = row_at(mass_ref, group, row)
            stiff_ref[at] = row_at(rigid_ref, group, row) * jnp.exp(0.5 * jnp.tanh(field))
            pull_ref[at] = (KICK * (1.0 + DECAY) * STIFF_SCALE) * mass
            push_ref[at] = KICK * (mass * row_at(load_ref, group, row))
        return carry

    lax.fori_loop(0, rows // SUBLANES, group_rows, 0)


def chain_kernel(
    slot_ref, pos_in, vel_in, stiff_ref, pull_ref, push_ref, gust_ref, out_ref,
    pos, vel, coarse_pos, coarse_vel, *, rows, far
):
    near = far - 2
    lane = lax.broadcasted_iota(jnp.int32, (SUBLANES, LANES), 1)
    sub = lax.broadcasted_iota(jnp.int32, (SUBLANES, LANES), 0)
    last_lane = lane == LANES - 1
    first_lane = lane == 0
    low_corner = last_lane & (sub == 0)
    high_corner = first_lane & (sub == SUBLANES - 1)
    half_pull = 1.0 / (1.0 + DECAY)
    slot = slot_ref[0]

    def gust(stage, step_index):
        return jnp.broadcast_to(gust_ref[stage, step_index:step_index + 1, :], (SUBLANES, LANES))

    def beside(row):
        below = jnp.where(last_lane, pltpu.roll(row, 1, 0), row)
        above = jnp.where(first_lane, pltpu.roll(row, SUBLANES - 1, 0), row)
        below = jnp.where(low_corner, 0.0, below)
        above = jnp.where(high_corner, 0.0, above)
        return pltpu.roll(below, 1, 1) + pltpu.roll(above, LANES - 1, 1)

    def sweep(source, margin, update):
        count = -(-(rows + 2 * margin) // UNROLL) * UNROLL
        first = min(-margin, rows + near - count)

        def weigh(row, before, here, after):
            return stiff_ref[row + far - 1] * (before + after + beside(here) - 4.0 * here)

        start = [source[first - 2 + far + i] for i in range(4)]
        carry = (
            weigh(first - 1, start[0], start[1], start[2]),
            weigh(first, start[1], start[2], start[3]),
            start[2],
            start[3],
        )

        def chunk(index, carry):
            base = first + index * UNROLL
            w_before, w_here, p_here, p_after = carry
            for j in range(UNROLL):
                p_next = source[base + j + 2 + far]
                w_after = weigh(base + j + 1, p_here, p_after, p_next)
                bent = w_before + w_after + beside(w_here) - 4.0 * w_here
                update(index, j, base + j, p_here, bent)
                w_before, w_here, p_here, p_after = w_here, w_after, p_after, p_next
            return w_before, w_here, p_here, p_after

        lax.fori_loop(0, count // UNROLL, chunk, carry)

    def start_slice(row, position, velocity, bent, gust_value):
        force = gust_value * push_ref[row + near] - half_pull * (pull_ref[row + near] * bent)
        shift = (TIME_STEP * DECAY) * velocity + force
        new_vel = COARSE_DECAY * velocity + (COARSE_SPAN / KICK) * force
        coarse_vel[row + near] = new_vel
        coarse_pos[row + near] = position + COARSE_SPAN * new_vel
        vel[row + near] = shift
        pos[row + far] = position + shift

    def advance(gust_value, joins):
        def update(index, j, row, position, bent):
            shift = (
                (DECAY * DECAY) * vel[row + near]
                + gust_value * push_ref[row + near]
                - pull_ref[row + near] * bent
            )
            vel[row + near] = shift
            moved = position + shift
            if joins:
                coarse = coarse_pos[row + near]
                moved = coarse + (moved - coarse)
            pos[row + far] = moved

        return update

    def end_velocity(row, bent, gust_value):
        force = gust_value * push_ref[row + near] - half_pull * (pull_ref[row + near] * bent)
        fine_vel = (1.0 / TIME_STEP) * (DECAY * vel[row + near] + force)
        coarse = coarse_vel[row + near]
        return coarse + (fine_vel - coarse)

    def finish(gust_value):
        def update(index, j, row, position, bent):
            group = index * (UNROLL // SUBLANES) + j // SUBLANES
            start = pl.multiple_of(group * SUBLANES * SUBLANES, SUBLANES * SUBLANES)
            at = start + j % SUBLANES
            out_ref[pl.ds(at, SUBLANES, stride=SUBLANES), :] = position
            out_ref[pl.ds(at + rows * SUBLANES, SUBLANES, stride=SUBLANES), :] = end_velocity(
                row, bent, gust_value
            )

        return update

    def fine_steps(stage, margin):
        for step_index in range(1, FINE):
            gust_value = DECAY * gust(stage, step_index - 1) + gust(stage, step_index)
            margin -= 2
            sweep(pos, margin, advance(gust_value, step_index == FINE - 1))
        return margin

    blank = jnp.zeros((SUBLANES, LANES), jnp.float32)
    for row in (-far, -far + 1, rows + far - 2, rows + far - 1):
        pos[row + far] = blank
    first_gust = gust(0, 0)
    sweep(
        pos_in,
        near,
        lambda index, j, row, position, bent: start_slice(
            row, position, vel_in[row + near], bent, first_gust
        ),
    )
    margin = fine_steps(0, near) - 2

    @pl.when(slot == 0)
    def _():
        sweep(pos, 0, finish(gust(0, FINE - 1)))

    @pl.when(slot != 0)
    def _():
        last_gust = gust(0, FINE - 1)
        next_gust = gust(1, 0)

        def link(index, j, row, position, bent):
            velocity = end_velocity(row, bent, last_gust)
            start_slice(row, position, velocity, bent, next_gust)

        sweep(pos, margin, link)
        fine_steps(1, margin)
        sweep(pos, 0, finish(gust(1, FINE - 1)))


def swap_pairs(count, first):
    pairs = [(i, i + 1) for i in range(first, count - 1, 2)]
    return pairs + [(target, source) for source, target in pairs]


def exchanged(low_rows, high_rows, odd):
    count = lax.axis_size("space")
    inner = lax.ppermute(jnp.where(odd, low_rows, high_rows), "space", swap_pairs(count, 0))
    outer = lax.ppermute(jnp.where(odd, high_rows, low_rows), "space", swap_pairs(count, 1))
    return jnp.where(odd, inner, outer), jnp.where(odd, outer, inner)


def in_vmem(count):
    return [pl.BlockSpec(memory_space=pltpu.VMEM)] * count


def in_smem(count):
    return [pl.BlockSpec(memory_space=pltpu.SMEM)] * count


def plane(count):
    return jax.ShapeDtypeStruct((count, SUBLANES, LANES), jnp.float32)


def two_slice_device(start_state, rigidity, inv_mass, gust_load, kl_coeff, gust_history):
    rows, cols = rigidity.shape
    far = 2 * (2 * FINE + 1)
    near = far - 2
    side = far + near
    time_slot = lax.axis_index("tm")
    space_slot = lax.axis_index("space")
    odd = space_slot % 2 == 1
    small = pltpu.CompilerParams(vmem_limit_bytes=16 * 2**20)

    edge_own, mid_own = pl.pallas_call(
        functools.partial(pack_kernel, rows=rows, far=far, near=near),
        out_shape=(plane(2 * side + 1), plane(2 * rows - 2 * side)),
        in_specs=in_smem(1) + in_vmem(1),
        out_specs=tuple(in_vmem(2)),
        compiler_params=small,
        name="pack",
    )(gust_history, tile_view(start_state))
    edge_in = passed_along(edge_own, "tm", 1)
    mid_in = passed_along(mid_own, "tm", 1)

    across = mode_table(space_slot * rows + jnp.arange(rows), rows * lax.axis_size("space"))
    along = mode_table(jnp.arange(cols), cols).reshape(KL, SUBLANES, LANES)
    stiff, pull, push = pl.pallas_call(
        field_kernel,
        out_shape=(plane(rows),) * 3,
        in_specs=in_smem(2) + in_vmem(4),
        out_specs=tuple(in_vmem(3)),
        compiler_params=small,
        name="field",
    )(kl_coeff, across, along, tile_view(rigidity), tile_view(inv_mass), tile_view(gust_load))
    wide = far - 1
    low, high = exchanged(
        jnp.concatenate([stiff[:wide], pull[:near], push[:near]]),
        jnp.concatenate([stiff[rows - wide:], pull[rows - near:], push[rows - near:]]),
        odd,
    )
    stiff = jnp.concatenate([low[:wide], stiff, high[:wide]])
    pull = jnp.concatenate([low[wide:wide + near], pull, high[wide:wide + near]])
    push = jnp.concatenate([low[wide + near:], push, high[wide + near:]])

    first = time_slot == 0
    edge = jnp.where(first, edge_own, edge_in)
    mid = jnp.where(first, mid_own, mid_in)
    low, high = exchanged(edge[:side], edge[side:2 * side], odd)
    inside = rows - 2 * far
    position = jnp.concatenate(
        [low[:far], edge[:far], mid[:inside], edge[side:side + far], high[:far]]
    )
    velocity = jnp.concatenate(
        [low[far:], edge[far:side], mid[inside:], edge[side + far:2 * side], high[far:]]
    )
    gusts = jnp.stack([edge[2 * side], edge_own[2 * side]])

    out = pl.pallas_call(
        functools.partial(chain_kernel, rows=rows, far=far),
        out_shape=jax.ShapeDtypeStruct((2 * rows * SUBLANES, LANES), jnp.float32),
        in_specs=in_smem(1) + in_vmem(6),
        out_specs=in_vmem(1)[0],
        scratch_shapes=[
            pltpu.VMEM((rows + 2 * far, SUBLANES, LANES), jnp.float32),
        ]
        + [pltpu.VMEM((rows + 2 * near, SUBLANES, LANES), jnp.float32)] * 3,
        compiler_params=small,
        name="chain",
    )(time_slot.reshape(1), position, velocity, stiff, pull, push, gusts)
    return from_tile_view(out, start_state.shape)


def chosen_device(start_state, rigidity, inv_mass, gust_load, kl_coeff, gust_history):
    rows, cols = rigidity.shape
    fits = cols == SUBLANES * LANES and rows % SUBLANES == 0 and rows > 4 * (2 * FINE + 1)
    two_slices = lax.axis_size("tm") == 2 and ITERS == 2 and start_state.shape[0] == 1
    device = two_slice_device if fits and two_slices else per_device
    return device(start_state, rigidity, inv_mass, gust_load, kl_coeff, gust_history)


def solution(mesh):
    in_specs = (
        P("tm", None, "space", None),
        P("space", None),
        P("space", None),
        P("space", None),
        P(),
        P("tm"),
    )
    out_specs = P("tm", None, "space", None)
    return jax.shard_map(
        chosen_device, mesh=mesh, in_specs=in_specs, out_specs=out_specs, check_vma=False
    )
```

```python
import functools

import jax
import jax.numpy as jnp
from jax import lax
from jax.experimental import pallas as pl
from jax.experimental.pallas import tpu as pltpu
from jax.sharding import PartitionSpec as P


FINE = 4
ITERS = 2
KL = 4


STIFF_SCALE = 1.0 / 64.0
TIME_STEP = 0.18
HALF_STEP = 0.09
DAMPING = 0.05


def extended(block, sides, width):
    for axis, dim in sides:
        count = lax.axis_size(axis)
        forward = [(i, i + 1) for i in range(count - 1)]
        backward = [(target, source) for source, target in forward]
        low = lax.ppermute(
            lax.slice_in_dim(block, block.shape[dim] - width, None, axis=dim), axis, forward
        )
        high = lax.ppermute(lax.slice_in_dim(block, 0, width, axis=dim), axis, backward)
        block = jnp.concatenate([low, block, high], axis=dim)
    return block


def passed_along(block, axis, distance):
    devices = range(lax.axis_size(axis))
    route = [(i - distance, i) for i in devices if i - distance in devices]
    return lax.ppermute(block, axis, route)


def laplace(padded):
    return (
        padded[2:, 1:-1]
        + padded[:-2, 1:-1]
        + padded[1:-1, 2:]
        + padded[1:-1, :-2]
        - 4.0 * padded[1:-1, 1:-1]
    )


def mode_table(positions, extent):
    orders = (jnp.arange(KL) + 1).astype(jnp.float32)
    coords = (positions.astype(jnp.float32) + 0.5) / extent
    return jnp.cos(jnp.pi * orders[:, None] * coords[None, :])


def build_rigidity(rigidity, kl_coeff, first_row, extent_rows, extent_cols):
    row_count = rigidity.shape[0]
    col_count = rigidity.shape[1]
    across = mode_table(first_row + jnp.arange(row_count), extent_rows)
    along_chord = mode_table(jnp.arange(col_count), extent_cols)
    mixed = jnp.dot(kl_coeff, along_chord, precision=lax.Precision.HIGHEST)
    kl_field = jnp.dot(across.T, mixed, precision=lax.Precision.HIGHEST)
    return rigidity * jnp.exp(0.5 * jnp.tanh(kl_field))


def apply_padded(widened, rigid_rim):
    weighted = rigid_rim * laplace(jnp.pad(widened, ((0, 0), (1, 1))))
    return STIFF_SCALE * laplace(jnp.pad(weighted, ((0, 0), (1, 1))))


def crop_rows(values_in, have_rim, want_rim):
    margin = have_rim - want_rim
    return values_in[margin : values_in.shape[0] - margin]


def accelerate(velocity, stiff_now, inv_mass, gust_load, gust_value):
    return inv_mass * (gust_load * gust_value - stiff_now) - DAMPING * velocity


def coarse_step(position, velocity, stiff_now, inv_mass, gust_load, gust_value):
    coarse_span = FINE * TIME_STEP
    new_vel = velocity + coarse_span * accelerate(
        velocity, stiff_now, inv_mass, gust_load, gust_value
    )
    return (position + coarse_span * new_vel, new_vel)


def per_device(start_state, rigidity, inv_mass, gust_load, kl_coeff, gust_history):
    row_count = rigidity.shape[0]
    col_count = rigidity.shape[1]
    space_count = lax.axis_size("space")
    time_count = lax.axis_size("tm")
    time_slot = lax.axis_index("tm")
    space_slot = lax.axis_index("space")
    stiff_field = build_rigidity(
        rigidity, kl_coeff, space_slot * row_count, row_count * space_count, col_count
    )
    reach = 2 * (FINE + 1)
    statics = extended(jnp.stack([stiff_field, inv_mass, gust_load]), (("space", 1),), reach)
    rigid_wide = statics[0]
    mass_wide = statics[1]
    load_wide = statics[2]
    rigid_one = crop_rows(rigid_wide, reach, 1)

    def coarse_stiff(moved):
        widened = extended(moved, (("space", 0),), 2)
        return apply_padded(widened, rigid_one)

    def coarse_move(position, velocity, stiff_now, gust_value):
        return coarse_step(position, velocity, stiff_now, inv_mass, gust_load, gust_value)

    position = start_state[0, 0]
    velocity = start_state[0, 1]
    end_pos = position
    end_vel = velocity
    for sweep_index in range(ITERS):
        last_sweep = sweep_index == ITERS - 1
        both = extended(jnp.stack([position, velocity]), (("space", 1),), reach)
        rim_now = reach
        fine_stiff_now = apply_padded(both[0], crop_rows(rigid_wide, reach, rim_now - 1))
        next_rim = rim_now - 2
        first_stiff = crop_rows(fine_stiff_now, next_rim, 0)
        pos_now = crop_rows(both[0], rim_now, next_rim)
        vel_now = crop_rows(both[1], rim_now, next_rim)
        rim_now = next_rim
        for step_index in range(FINE):
            fine_gust_value = gust_history[step_index]
            mass_now = crop_rows(mass_wide, reach, rim_now)
            load_now = crop_rows(load_wide, reach, rim_now)
            half_vel = vel_now + HALF_STEP * accelerate(
                vel_now, fine_stiff_now, mass_now, load_now, fine_gust_value
            )
            pos_now = pos_now + TIME_STEP * half_vel
            fine_stiff_now = apply_padded(pos_now, crop_rows(rigid_wide, reach, rim_now - 1))
            next_rim = rim_now - 2
            pos_now = crop_rows(pos_now, rim_now, next_rim)
            half_vel = crop_rows(half_vel, rim_now, next_rim)
            mass_now = crop_rows(mass_wide, reach, next_rim)
            load_now = crop_rows(load_wide, reach, next_rim)
            vel_now = half_vel + HALF_STEP * accelerate(
                half_vel, fine_stiff_now, mass_now, load_now, fine_gust_value
            )
            rim_now = next_rim
        fine_pos, fine_vel, first_stiff = (pos_now, vel_now, first_stiff)
        coarse_pos, coarse_vel = coarse_move(position, velocity, first_stiff, gust_history[0])
        delta_pos = fine_pos - coarse_pos
        delta_vel = fine_vel - coarse_vel
        chain_pos = position
        chain_vel = velocity
        for turn_index in range(1, time_count):
            stiff_now = coarse_stiff(chain_pos)
            moved_pos, moved_vel = coarse_move(chain_pos, chain_vel, stiff_now, gust_history[0])
            outgoing = jnp.stack([moved_pos + delta_pos, moved_vel + delta_vel])
            arrived = passed_along(outgoing, "tm", 1)
            chain_pos = jnp.where(time_slot == turn_index, arrived[0], chain_pos)
            chain_vel = jnp.where(time_slot == turn_index, arrived[1], chain_vel)
        if last_sweep:
            stiff_now = coarse_stiff(chain_pos)
            moved_pos, moved_vel = coarse_move(chain_pos, chain_vel, stiff_now, gust_history[0])
            end_pos = moved_pos + delta_pos
            end_vel = moved_vel + delta_vel
        position = chain_pos
        velocity = chain_vel
    return jnp.stack([end_pos, end_vel])[None]


LANES = 128
SUBLANES = 8
COARSE_SPAN = FINE * TIME_STEP
DECAY = 1.0 - HALF_STEP * DAMPING
COARSE_DECAY = 1.0 - COARSE_SPAN * DAMPING
KICK = TIME_STEP * HALF_STEP
UNROLL = 32


def tile_view(block):
    width = block.shape[-1] // LANES
    tiles = block.reshape(-1, SUBLANES, width, LANES).transpose(0, 2, 1, 3)
    return tiles.reshape(-1, LANES)


def from_tile_view(view, shape):
    width = shape[-1] // LANES
    tiles = view.reshape(-1, width, SUBLANES, LANES).transpose(0, 2, 1, 3)
    return tiles.reshape(shape)


def row_at(view_ref, group, row):
    start = pl.multiple_of(group * SUBLANES * SUBLANES, SUBLANES * SUBLANES)
    return view_ref[pl.ds(start + row, SUBLANES, stride=SUBLANES), :]


def pack_kernel(gust_ref, view_ref, edge_ref, mid_ref, *, rows, far, near):
    sub = lax.broadcasted_iota(jnp.int32, (SUBLANES, LANES), 0)
    gusts = jnp.zeros((SUBLANES, LANES), jnp.float32)
    for step_index in range(FINE):
        gusts = jnp.where(sub == step_index, gust_ref[step_index], gusts)
    side = far + near
    edge_ref[2 * side] = gusts
    for part, width, at in ((0, far, 0), (1, near, far)):
        for row in range(rows):
            group = (part * rows + row) // SUBLANES
            value = row_at(view_ref, group, row % SUBLANES)
            if row < width:
                edge_ref[at + row] = value
            elif row >= rows - width:
                edge_ref[side + at + row - (rows - width)] = value
            else:
                mid_ref[part * (rows - 2 * far) + row - width] = value


def field_kernel(
    kl_ref, across_ref, along_ref, rigid_ref, mass_ref, load_ref, stiff_ref, pull_ref, push_ref
):
    rows = stiff_ref.shape[0]
    mixed = []
    for order in range(KL):
        total = kl_ref[order, 0] * along_ref[0]
        for other in range(1, KL):
            total = total + kl_ref[order, other] * along_ref[other]
        mixed.append(total)

    def group_rows(group, carry):
        for row in range(SUBLANES):
            at = group * SUBLANES + row
            field = across_ref[0, at] * mixed[0]
            for order in range(1, KL):
                field = field + across_ref[order, at] * mixed[order]
            mass = row_at(mass_ref, group, row)
            stiff_ref[at] = row_at(rigid_ref, group, row) * jnp.exp(0.5 * jnp.tanh(field))
            pull_ref[at] = (KICK * (1.0 + DECAY) * STIFF_SCALE) * mass
            push_ref[at] = KICK * (mass * row_at(load_ref, group, row))
        return carry

    lax.fori_loop(0, rows // SUBLANES, group_rows, 0)


def chain_kernel(
    slot_ref, pos_in, vel_in, stiff_ref, pull_ref, push_ref, gust_ref, out_ref,
    pos, vel, coarse_pos, coarse_vel, *, rows, far
):
    near = far - 2
    lane = lax.broadcasted_iota(jnp.int32, (SUBLANES, LANES), 1)
    sub = lax.broadcasted_iota(jnp.int32, (SUBLANES, LANES), 0)
    last_lane = lane == LANES - 1
    first_lane = lane == 0
    low_corner = last_lane & (sub == 0)
    high_corner = first_lane & (sub == SUBLANES - 1)
    half_pull = 1.0 / (1.0 + DECAY)
    slot = slot_ref[0]

    def gust(stage, step_index):
        return jnp.broadcast_to(gust_ref[stage, step_index:step_index + 1, :], (SUBLANES, LANES))

    def beside(row):
        below = jnp.where(last_lane, pltpu.roll(row, 1, 0), row)
        above = jnp.where(first_lane, pltpu.roll(row, SUBLANES - 1, 0), row)
        below = jnp.where(low_corner, 0.0, below)
        above = jnp.where(high_corner, 0.0, above)
        return pltpu.roll(below, 1, 1) + pltpu.roll(above, LANES - 1, 1)

    def sweep(source, margin, update):
        count = -(-(rows + 2 * margin) // UNROLL) * UNROLL
        first = min(-margin, rows + near - count)

        def weigh(row, before, here, after):
            return stiff_ref[row + far - 1] * (before + after + beside(here) - 4.0 * here)

        start = [source[first - 2 + far + i] for i in range(4)]
        carry = (
            weigh(first - 1, start[0], start[1], start[2]),
            weigh(first, start[1], start[2], start[3]),
            start[2],
            start[3],
        )

        def chunk(index, carry):
            base = first + index * UNROLL
            w_before, w_here, p_here, p_after = carry
            for j in range(UNROLL):
                p_next = source[base + j + 2 + far]
                w_after = weigh(base + j + 1, p_here, p_after, p_next)
                bent = w_before + w_after + beside(w_here) - 4.0 * w_here
                update(index, j, base + j, p_here, bent)
                w_before, w_here, p_here, p_after = w_here, w_after, p_after, p_next
            return w_before, w_here, p_here, p_after

        lax.fori_loop(0, count // UNROLL, chunk, carry)

    def start_slice(row, position, velocity, bent, gust_value):
        force = gust_value * push_ref[row + near] - half_pull * (pull_ref[row + near] * bent)
        shift = (TIME_STEP * DECAY) * velocity + force
        new_vel = COARSE_DECAY * velocity + (COARSE_SPAN / KICK) * force
        coarse_vel[row + near] = new_vel
        coarse_pos[row + near] = position + COARSE_SPAN * new_vel
        vel[row + near] = shift
        pos[row + far] = position + shift

    def advance(gust_value, joins):
        def update(index, j, row, position, bent):
            shift = (
                (DECAY * DECAY) * vel[row + near]
                + gust_value * push_ref[row + near]
                - pull_ref[row + near] * bent
            )
            vel[row + near] = shift
            moved = position + shift
            if joins:
                coarse = coarse_pos[row + near]
                moved = coarse + (moved - coarse)
            pos[row + far] = moved

        return update

    def end_velocity(row, bent, gust_value):
        force = gust_value * push_ref[row + near] - half_pull * (pull_ref[row + near] * bent)
        fine_vel = (1.0 / TIME_STEP) * (DECAY * vel[row + near] + force)
        coarse = coarse_vel[row + near]
        return coarse + (fine_vel - coarse)

    def finish(gust_value):
        def update(index, j, row, position, bent):
            group = index * (UNROLL // SUBLANES) + j // SUBLANES
            start = pl.multiple_of(group * SUBLANES * SUBLANES, SUBLANES * SUBLANES)
            at = start + j % SUBLANES
            out_ref[pl.ds(at, SUBLANES, stride=SUBLANES), :] = position
            out_ref[pl.ds(at + rows * SUBLANES, SUBLANES, stride=SUBLANES), :] = end_velocity(
                row, bent, gust_value
            )

        return update

    def fine_steps(stage, margin):
        for step_index in range(1, FINE):
            gust_value = DECAY * gust(stage, step_index - 1) + gust(stage, step_index)
            margin -= 2
            sweep(pos, margin, advance(gust_value, step_index == FINE - 1))
        return margin

    blank = jnp.zeros((SUBLANES, LANES), jnp.float32)
    for row in (-far, -far + 1, rows + far - 2, rows + far - 1):
        pos[row + far] = blank
    first_gust = gust(0, 0)
    sweep(
        pos_in,
        near,
        lambda index, j, row, position, bent: start_slice(
            row, position, vel_in[row + near], bent, first_gust
        ),
    )
    margin = fine_steps(0, near) - 2

    @pl.when(slot == 0)
    def _():
        sweep(pos, 0, finish(gust(0, FINE - 1)))

    @pl.when(slot != 0)
    def _():
        last_gust = gust(0, FINE - 1)
        next_gust = gust(1, 0)

        def link(index, j, row, position, bent):
            velocity = end_velocity(row, bent, last_gust)
            start_slice(row, position, velocity, bent, next_gust)

        sweep(pos, margin, link)
        fine_steps(1, margin)
        sweep(pos, 0, finish(gust(1, FINE - 1)))


def swap_pairs(count, first):
    pairs = [(i, i + 1) for i in range(first, count - 1, 2)]
    return pairs + [(target, source) for source, target in pairs]


def exchanged(low_rows, high_rows, odd):
    count = lax.axis_size("space")
    inner = lax.ppermute(jnp.where(odd, low_rows, high_rows), "space", swap_pairs(count, 0))
    outer = lax.ppermute(jnp.where(odd, high_rows, low_rows), "space", swap_pairs(count, 1))
    return jnp.where(odd, inner, outer), jnp.where(odd, outer, inner)


def in_vmem(count):
    return [pl.BlockSpec(memory_space=pltpu.VMEM)] * count


def in_smem(count):
    return [pl.BlockSpec(memory_space=pltpu.SMEM)] * count


def plane(count):
    return jax.ShapeDtypeStruct((count, SUBLANES, LANES), jnp.float32)


def field_call(kl_coeff, across, along, rigidity, inv_mass, gust_load):
    rows = rigidity.shape[0] // SUBLANES
    return pl.pallas_call(
        field_kernel,
        out_shape=(plane(rows),) * 3,
        in_specs=in_smem(2) + in_vmem(4),
        out_specs=tuple(in_vmem(3)),
        compiler_params=pltpu.CompilerParams(vmem_limit_bytes=16 * 2**20),
        name="field",
    )(kl_coeff, across, along, rigidity, inv_mass, gust_load)


def chain_call(slot, position, velocity, stiff, pull, push, gusts, rows, far):
    near = far - 2
    return pl.pallas_call(
        functools.partial(chain_kernel, rows=rows, far=far),
        out_shape=jax.ShapeDtypeStruct((2 * rows * SUBLANES, LANES), jnp.float32),
        in_specs=in_smem(1) + in_vmem(6),
        out_specs=in_vmem(1)[0],
        scratch_shapes=[pltpu.VMEM((rows + 2 * far, SUBLANES, LANES), jnp.float32)]
        + [pltpu.VMEM((rows + 2 * near, SUBLANES, LANES), jnp.float32)] * 3,
        compiler_params=pltpu.CompilerParams(vmem_limit_bytes=16 * 2**20),
        name="chain",
    )(slot, position, velocity, stiff, pull, push, gusts)


def two_slice_device(start_state, rigidity, inv_mass, gust_load, kl_coeff, gust_history):
    rows, cols = rigidity.shape
    far = 2 * (2 * FINE + 1)
    near = far - 2
    side = far + near
    time_slot = lax.axis_index("tm")
    space_slot = lax.axis_index("space")
    odd = space_slot % 2 == 1
    small = pltpu.CompilerParams(vmem_limit_bytes=16 * 2**20)

    edge_own, mid_own = pl.pallas_call(
        functools.partial(pack_kernel, rows=rows, far=far, near=near),
        out_shape=(plane(2 * side + 1), plane(2 * rows - 2 * side)),
        in_specs=in_smem(1) + in_vmem(1),
        out_specs=tuple(in_vmem(2)),
        compiler_params=small,
        name="pack",
    )(gust_history, tile_view(start_state))
    edge_in = passed_along(edge_own, "tm", 1)
    mid_in = passed_along(mid_own, "tm", 1)
    edge_own, rigidity, inv_mass, gust_load = lax.optimization_barrier(
        (edge_own, rigidity, inv_mass, gust_load)
    )

    across = mode_table(space_slot * rows + jnp.arange(rows), rows * lax.axis_size("space"))
    along = mode_table(jnp.arange(cols), cols).reshape(KL, SUBLANES, LANES)
    stiff, pull, push = field_call(
        kl_coeff, across, along, tile_view(rigidity), tile_view(inv_mass), tile_view(gust_load)
    )
    wide = far - 1
    low, high = exchanged(
        jnp.concatenate([stiff[:wide], pull[:near], push[:near]]),
        jnp.concatenate([stiff[rows - wide:], pull[rows - near:], push[rows - near:]]),
        odd,
    )
    stiff = jnp.concatenate([low[:wide], stiff, high[:wide]])
    pull = jnp.concatenate([low[wide:wide + near], pull, high[wide:wide + near]])
    push = jnp.concatenate([low[wide + near:], push, high[wide + near:]])

    first = time_slot == 0
    edge = jnp.where(first, edge_own, edge_in)
    mid = jnp.where(first, mid_own, mid_in)
    low, high = exchanged(edge[:side], edge[side:2 * side], odd)
    inside = rows - 2 * far
    position = jnp.concatenate(
        [low[:far], edge[:far], mid[:inside], edge[side:side + far], high[:far]]
    )
    velocity = jnp.concatenate(
        [low[far:], edge[far:side], mid[inside:], edge[side + far:2 * side], high[far:]]
    )
    gusts = jnp.stack([edge[2 * side], edge_own[2 * side]])

    out = chain_call(
        time_slot.reshape(1), position, velocity, stiff, pull, push, gusts, rows, far
    )
    return from_tile_view(out, start_state.shape)


def layered_device(*args):
    return two_slice_device(*args)


def chosen_device(start_state, rigidity, inv_mass, gust_load, kl_coeff, gust_history):
    rows, cols = rigidity.shape
    fits = cols == SUBLANES * LANES and rows % SUBLANES == 0 and rows > 4 * (2 * FINE + 1)
    two_slices = lax.axis_size("tm") == 2 and ITERS == 2 and start_state.shape[0] == 1
    device = layered_device if fits and two_slices else per_device
    return device(start_state, rigidity, inv_mass, gust_load, kl_coeff, gust_history)


def solution(mesh):
    in_specs = (
        P("tm", None, "space", None),
        P("space", None),
        P("space", None),
        P("space", None),
        P(),
        P("tm"),
    )
    out_specs = P("tm", None, "space", None)
    return jax.shard_map(
        chosen_device, mesh=mesh, in_specs=in_specs, out_specs=out_specs, check_vma=False
    )
```

```python
import functools

import jax
import jax.numpy as jnp
from jax import lax
from jax.experimental import pallas as pl
from jax.experimental.pallas import tpu as pltpu
from jax.sharding import PartitionSpec as P


FINE = 4
ITERS = 2
KL = 4


STIFF_SCALE = 1.0 / 64.0
TIME_STEP = 0.18
HALF_STEP = 0.09
DAMPING = 0.05


def extended(block, sides, width):
    for axis, dim in sides:
        count = lax.axis_size(axis)
        forward = [(i, i + 1) for i in range(count - 1)]
        backward = [(target, source) for source, target in forward]
        low = lax.ppermute(
            lax.slice_in_dim(block, block.shape[dim] - width, None, axis=dim), axis, forward
        )
        high = lax.ppermute(lax.slice_in_dim(block, 0, width, axis=dim), axis, backward)
        block = jnp.concatenate([low, block, high], axis=dim)
    return block


def passed_along(block, axis, distance):
    devices = range(lax.axis_size(axis))
    route = [(i - distance, i) for i in devices if i - distance in devices]
    return lax.ppermute(block, axis, route)


def laplace(padded):
    return (
        padded[2:, 1:-1]
        + padded[:-2, 1:-1]
        + padded[1:-1, 2:]
        + padded[1:-1, :-2]
        - 4.0 * padded[1:-1, 1:-1]
    )


def mode_table(positions, extent):
    orders = (jnp.arange(KL) + 1).astype(jnp.float32)
    coords = (positions.astype(jnp.float32) + 0.5) / extent
    return jnp.cos(jnp.pi * orders[:, None] * coords[None, :])


def build_rigidity(rigidity, kl_coeff, first_row, extent_rows, extent_cols):
    row_count = rigidity.shape[0]
    col_count = rigidity.shape[1]
    across = mode_table(first_row + jnp.arange(row_count), extent_rows)
    along_chord = mode_table(jnp.arange(col_count), extent_cols)
    mixed = jnp.dot(kl_coeff, along_chord, precision=lax.Precision.HIGHEST)
    kl_field = jnp.dot(across.T, mixed, precision=lax.Precision.HIGHEST)
    return rigidity * jnp.exp(0.5 * jnp.tanh(kl_field))


def apply_padded(widened, rigid_rim):
    weighted = rigid_rim * laplace(jnp.pad(widened, ((0, 0), (1, 1))))
    return STIFF_SCALE * laplace(jnp.pad(weighted, ((0, 0), (1, 1))))


def crop_rows(values_in, have_rim, want_rim):
    margin = have_rim - want_rim
    return values_in[margin : values_in.shape[0] - margin]


def accelerate(velocity, stiff_now, inv_mass, gust_load, gust_value):
    return inv_mass * (gust_load * gust_value - stiff_now) - DAMPING * velocity


def coarse_step(position, velocity, stiff_now, inv_mass, gust_load, gust_value):
    coarse_span = FINE * TIME_STEP
    new_vel = velocity + coarse_span * accelerate(
        velocity, stiff_now, inv_mass, gust_load, gust_value
    )
    return (position + coarse_span * new_vel, new_vel)


def per_device(start_state, rigidity, inv_mass, gust_load, kl_coeff, gust_history):
    row_count = rigidity.shape[0]
    col_count = rigidity.shape[1]
    space_count = lax.axis_size("space")
    time_count = lax.axis_size("tm")
    time_slot = lax.axis_index("tm")
    space_slot = lax.axis_index("space")
    stiff_field = build_rigidity(
        rigidity, kl_coeff, space_slot * row_count, row_count * space_count, col_count
    )
    reach = 2 * (FINE + 1)
    statics = extended(jnp.stack([stiff_field, inv_mass, gust_load]), (("space", 1),), reach)
    rigid_wide = statics[0]
    mass_wide = statics[1]
    load_wide = statics[2]
    rigid_one = crop_rows(rigid_wide, reach, 1)

    def coarse_stiff(moved):
        widened = extended(moved, (("space", 0),), 2)
        return apply_padded(widened, rigid_one)

    def coarse_move(position, velocity, stiff_now, gust_value):
        return coarse_step(position, velocity, stiff_now, inv_mass, gust_load, gust_value)

    position = start_state[0, 0]
    velocity = start_state[0, 1]
    end_pos = position
    end_vel = velocity
    for sweep_index in range(ITERS):
        last_sweep = sweep_index == ITERS - 1
        both = extended(jnp.stack([position, velocity]), (("space", 1),), reach)
        rim_now = reach
        fine_stiff_now = apply_padded(both[0], crop_rows(rigid_wide, reach, rim_now - 1))
        next_rim = rim_now - 2
        first_stiff = crop_rows(fine_stiff_now, next_rim, 0)
        pos_now = crop_rows(both[0], rim_now, next_rim)
        vel_now = crop_rows(both[1], rim_now, next_rim)
        rim_now = next_rim
        for step_index in range(FINE):
            fine_gust_value = gust_history[step_index]
            mass_now = crop_rows(mass_wide, reach, rim_now)
            load_now = crop_rows(load_wide, reach, rim_now)
            half_vel = vel_now + HALF_STEP * accelerate(
                vel_now, fine_stiff_now, mass_now, load_now, fine_gust_value
            )
            pos_now = pos_now + TIME_STEP * half_vel
            fine_stiff_now = apply_padded(pos_now, crop_rows(rigid_wide, reach, rim_now - 1))
            next_rim = rim_now - 2
            pos_now = crop_rows(pos_now, rim_now, next_rim)
            half_vel = crop_rows(half_vel, rim_now, next_rim)
            mass_now = crop_rows(mass_wide, reach, next_rim)
            load_now = crop_rows(load_wide, reach, next_rim)
            vel_now = half_vel + HALF_STEP * accelerate(
                half_vel, fine_stiff_now, mass_now, load_now, fine_gust_value
            )
            rim_now = next_rim
        fine_pos, fine_vel, first_stiff = (pos_now, vel_now, first_stiff)
        coarse_pos, coarse_vel = coarse_move(position, velocity, first_stiff, gust_history[0])
        delta_pos = fine_pos - coarse_pos
        delta_vel = fine_vel - coarse_vel
        chain_pos = position
        chain_vel = velocity
        for turn_index in range(1, time_count):
            stiff_now = coarse_stiff(chain_pos)
            moved_pos, moved_vel = coarse_move(chain_pos, chain_vel, stiff_now, gust_history[0])
            outgoing = jnp.stack([moved_pos + delta_pos, moved_vel + delta_vel])
            arrived = passed_along(outgoing, "tm", 1)
            chain_pos = jnp.where(time_slot == turn_index, arrived[0], chain_pos)
            chain_vel = jnp.where(time_slot == turn_index, arrived[1], chain_vel)
        if last_sweep:
            stiff_now = coarse_stiff(chain_pos)
            moved_pos, moved_vel = coarse_move(chain_pos, chain_vel, stiff_now, gust_history[0])
            end_pos = moved_pos + delta_pos
            end_vel = moved_vel + delta_vel
        position = chain_pos
        velocity = chain_vel
    return jnp.stack([end_pos, end_vel])[None]


LANES = 128
SUBLANES = 8
COARSE_SPAN = FINE * TIME_STEP
DECAY = 1.0 - HALF_STEP * DAMPING
COARSE_DECAY = 1.0 - COARSE_SPAN * DAMPING
KICK = TIME_STEP * HALF_STEP
UNROLL = 32


def tile_view(block):
    width = block.shape[-1] // LANES
    tiles = block.reshape(-1, SUBLANES, width, LANES).transpose(0, 2, 1, 3)
    return tiles.reshape(-1, LANES)


def from_tile_view(view, shape):
    width = shape[-1] // LANES
    tiles = view.reshape(-1, width, SUBLANES, LANES).transpose(0, 2, 1, 3)
    return tiles.reshape(shape)


def row_at(view_ref, group, row):
    start = pl.multiple_of(group * SUBLANES * SUBLANES, SUBLANES * SUBLANES)
    return view_ref[pl.ds(start + row, SUBLANES, stride=SUBLANES), :]


def pack_kernel(
    gust_hbm, view_hbm, edge_ref, mid_ref, view_ref, gust_ref, sems, *, rows, far, near
):
    gust_copy = pltpu.make_async_copy(gust_hbm, gust_ref, sems.at[2])
    half = rows * SUBLANES
    copies = []
    for part in range(2):
        piece = pl.ds(part * half, half)
        copies.append(
            pltpu.make_async_copy(view_hbm.at[piece], view_ref.at[piece], sems.at[part])
        )
        copies[part].start()
    gust_copy.start()
    side = far + near
    for part, width, at in ((0, far, 0), (1, near, far)):
        copies[part].wait()
        for row in range(rows):
            group = (part * rows + row) // SUBLANES
            value = row_at(view_ref, group, row % SUBLANES)
            if row < width:
                edge_ref[at + row] = value
            elif row >= rows - width:
                edge_ref[side + at + row - (rows - width)] = value
            else:
                mid_ref[part * (rows - 2 * far) + row - width] = value
    gust_copy.wait()
    sub = lax.broadcasted_iota(jnp.int32, (SUBLANES, LANES), 0)
    gusts = jnp.zeros((SUBLANES, LANES), jnp.float32)
    for step_index in range(FINE):
        gusts = jnp.where(sub == step_index, gust_ref[step_index], gusts)
    edge_ref[2 * side] = gusts


def field_kernel(
    kl_ref, across_ref, along_ref, rigid_ref, mass_ref, load_ref, stiff_ref, pull_ref, push_ref
):
    rows = stiff_ref.shape[0]
    mixed = []
    for order in range(KL):
        total = kl_ref[order, 0] * along_ref[0]
        for other in range(1, KL):
            total = total + kl_ref[order, other] * along_ref[other]
        mixed.append(total)

    def group_rows(group, carry):
        for row in range(SUBLANES):
            at = group * SUBLANES + row
            field = across_ref[0, at] * mixed[0]
            for order in range(1, KL):
                field = field + across_ref[order, at] * mixed[order]
            mass = row_at(mass_ref, group, row)
            stiff_ref[at] = row_at(rigid_ref, group, row) * jnp.exp(0.5 * jnp.tanh(field))
            pull_ref[at] = (KICK * (1.0 + DECAY) * STIFF_SCALE) * mass
            push_ref[at] = KICK * (mass * row_at(load_ref, group, row))
        return carry

    lax.fori_loop(0, rows // SUBLANES, group_rows, 0)


def chain_kernel(
    slot_ref, pos_in, vel_in, stiff_ref, pull_ref, push_ref, gust_ref, out_ref,
    pos, vel, coarse_pos, coarse_vel, *, rows, far
):
    near = far - 2
    lane = lax.broadcasted_iota(jnp.int32, (SUBLANES, LANES), 1)
    sub = lax.broadcasted_iota(jnp.int32, (SUBLANES, LANES), 0)
    last_lane = lane == LANES - 1
    first_lane = lane == 0
    low_corner = last_lane & (sub == 0)
    high_corner = first_lane & (sub == SUBLANES - 1)
    half_pull = 1.0 / (1.0 + DECAY)
    slot = slot_ref[0]

    def gust(stage, step_index):
        return jnp.broadcast_to(gust_ref[stage, step_index:step_index + 1, :], (SUBLANES, LANES))

    def beside(row):
        below = jnp.where(last_lane, pltpu.roll(row, 1, 0), row)
        above = jnp.where(first_lane, pltpu.roll(row, SUBLANES - 1, 0), row)
        below = jnp.where(low_corner, 0.0, below)
        above = jnp.where(high_corner, 0.0, above)
        return pltpu.roll(below, 1, 1) + pltpu.roll(above, LANES - 1, 1)

    def sweep(source, margin, update):
        count = -(-(rows + 2 * margin) // UNROLL) * UNROLL
        first = min(-margin, rows + near - count)

        def weigh(row, before, here, after):
            return stiff_ref[row + far - 1] * (before + after + beside(here) - 4.0 * here)

        start = [source[first - 2 + far + i] for i in range(4)]
        carry = (
            weigh(first - 1, start[0], start[1], start[2]),
            weigh(first, start[1], start[2], start[3]),
            start[2],
            start[3],
        )

        def chunk(index, carry):
            base = first + index * UNROLL
            w_before, w_here, p_here, p_after = carry
            for j in range(UNROLL):
                p_next = source[base + j + 2 + far]
                w_after = weigh(base + j + 1, p_here, p_after, p_next)
                bent = w_before + w_after + beside(w_here) - 4.0 * w_here
                update(index, j, base + j, p_here, bent)
                w_before, w_here, p_here, p_after = w_here, w_after, p_after, p_next
            return w_before, w_here, p_here, p_after

        lax.fori_loop(0, count // UNROLL, chunk, carry)

    def start_slice(row, position, velocity, bent, gust_value):
        force = gust_value * push_ref[row + near] - half_pull * (pull_ref[row + near] * bent)
        shift = (TIME_STEP * DECAY) * velocity + force
        new_vel = COARSE_DECAY * velocity + (COARSE_SPAN / KICK) * force
        coarse_vel[row + near] = new_vel
        coarse_pos[row + near] = position + COARSE_SPAN * new_vel
        vel[row + near] = shift
        pos[row + far] = position + shift

    def advance(gust_value, joins):
        def update(index, j, row, position, bent):
            shift = (
                (DECAY * DECAY) * vel[row + near]
                + gust_value * push_ref[row + near]
                - pull_ref[row + near] * bent
            )
            vel[row + near] = shift
            moved = position + shift
            if joins:
                coarse = coarse_pos[row + near]
                moved = coarse + (moved - coarse)
            pos[row + far] = moved

        return update

    def end_velocity(row, bent, gust_value):
        force = gust_value * push_ref[row + near] - half_pull * (pull_ref[row + near] * bent)
        fine_vel = (1.0 / TIME_STEP) * (DECAY * vel[row + near] + force)
        coarse = coarse_vel[row + near]
        return coarse + (fine_vel - coarse)

    def finish(gust_value):
        def update(index, j, row, position, bent):
            group = index * (UNROLL // SUBLANES) + j // SUBLANES
            start = pl.multiple_of(group * SUBLANES * SUBLANES, SUBLANES * SUBLANES)
            at = start + j % SUBLANES
            out_ref[pl.ds(at, SUBLANES, stride=SUBLANES), :] = position
            out_ref[pl.ds(at + rows * SUBLANES, SUBLANES, stride=SUBLANES), :] = end_velocity(
                row, bent, gust_value
            )

        return update

    def fine_steps(stage, margin):
        for step_index in range(1, FINE):
            gust_value = DECAY * gust(stage, step_index - 1) + gust(stage, step_index)
            margin -= 2
            sweep(pos, margin, advance(gust_value, step_index == FINE - 1))
        return margin

    blank = jnp.zeros((SUBLANES, LANES), jnp.float32)
    for row in (-far, -far + 1, rows + far - 2, rows + far - 1):
        pos[row + far] = blank
    first_gust = gust(0, 0)
    sweep(
        pos_in,
        near,
        lambda index, j, row, position, bent: start_slice(
            row, position, vel_in[row + near], bent, first_gust
        ),
    )
    margin = fine_steps(0, near) - 2

    @pl.when(slot == 0)
    def _():
        sweep(pos, 0, finish(gust(0, FINE - 1)))

    @pl.when(slot != 0)
    def _():
        last_gust = gust(0, FINE - 1)
        next_gust = gust(1, 0)

        def link(index, j, row, position, bent):
            velocity = end_velocity(row, bent, last_gust)
            start_slice(row, position, velocity, bent, next_gust)

        sweep(pos, margin, link)
        fine_steps(1, margin)
        sweep(pos, 0, finish(gust(1, FINE - 1)))


def swap_pairs(count, first):
    pairs = [(i, i + 1) for i in range(first, count - 1, 2)]
    return pairs + [(target, source) for source, target in pairs]


def exchanged(low_rows, high_rows, odd):
    count = lax.axis_size("space")
    inner = lax.ppermute(jnp.where(odd, low_rows, high_rows), "space", swap_pairs(count, 0))
    outer = lax.ppermute(jnp.where(odd, high_rows, low_rows), "space", swap_pairs(count, 1))
    return jnp.where(odd, inner, outer), jnp.where(odd, outer, inner)


def in_vmem(count):
    return [pl.BlockSpec(memory_space=pltpu.VMEM)] * count


def in_smem(count):
    return [pl.BlockSpec(memory_space=pltpu.SMEM)] * count


def in_hbm(array):
    return pltpu.with_memory_space_constraint(array, pltpu.HBM)


def plane(count):
    return jax.ShapeDtypeStruct((count, SUBLANES, LANES), jnp.float32)


def field_call(kl_coeff, across, along, rigidity, inv_mass, gust_load):
    rows = rigidity.shape[0] // SUBLANES
    return pl.pallas_call(
        field_kernel,
        out_shape=(plane(rows),) * 3,
        in_specs=in_smem(2) + in_vmem(4),
        out_specs=tuple(in_vmem(3)),
        compiler_params=pltpu.CompilerParams(vmem_limit_bytes=16 * 2**20),
        name="field",
    )(kl_coeff, across, along, rigidity, inv_mass, gust_load)


def chain_call(slot, position, velocity, stiff, pull, push, gusts, rows, far):
    near = far - 2
    return pl.pallas_call(
        functools.partial(chain_kernel, rows=rows, far=far),
        out_shape=jax.ShapeDtypeStruct((2 * rows * SUBLANES, LANES), jnp.float32),
        in_specs=in_smem(1) + in_vmem(6),
        out_specs=in_vmem(1)[0],
        scratch_shapes=[pltpu.VMEM((rows + 2 * far, SUBLANES, LANES), jnp.float32)]
        + [pltpu.VMEM((rows + 2 * near, SUBLANES, LANES), jnp.float32)] * 3,
        compiler_params=pltpu.CompilerParams(vmem_limit_bytes=16 * 2**20),
        name="chain",
    )(slot, position, velocity, stiff, pull, push, gusts)


def two_slice_device(start_state, rigidity, inv_mass, gust_load, kl_coeff, gust_history):
    rows, cols = rigidity.shape
    far = 2 * (2 * FINE + 1)
    near = far - 2
    side = far + near
    time_slot = lax.axis_index("tm")
    space_slot = lax.axis_index("space")
    odd = space_slot % 2 == 1
    small = pltpu.CompilerParams(vmem_limit_bytes=16 * 2**20)

    edge_own, mid_own = pl.pallas_call(
        functools.partial(pack_kernel, rows=rows, far=far, near=near),
        out_shape=(plane(2 * side + 1), plane(2 * rows - 2 * side)),
        in_specs=[pl.BlockSpec(memory_space=pltpu.HBM)] * 2,
        out_specs=tuple(in_vmem(2)),
        scratch_shapes=[
            pltpu.VMEM((2 * rows * SUBLANES, LANES), jnp.float32),
            pltpu.SMEM((FINE,), jnp.float32),
            pltpu.SemaphoreType.DMA((3,)),
        ],
        compiler_params=small,
        name="pack",
    )(in_hbm(gust_history), in_hbm(tile_view(start_state)))
    edge_in = passed_along(edge_own, "tm", 1)
    mid_in = passed_along(mid_own, "tm", 1)
    edge_own, rigidity, inv_mass, gust_load = lax.optimization_barrier(
        (edge_own, rigidity, inv_mass, gust_load)
    )

    across = mode_table(space_slot * rows + jnp.arange(rows), rows * lax.axis_size("space"))
    along = mode_table(jnp.arange(cols), cols).reshape(KL, SUBLANES, LANES)
    stiff, pull, push = field_call(
        kl_coeff, across, along, tile_view(rigidity), tile_view(inv_mass), tile_view(gust_load)
    )
    wide = far - 1
    low, high = exchanged(
        jnp.concatenate([stiff[:wide], pull[:near], push[:near]]),
        jnp.concatenate([stiff[rows - wide:], pull[rows - near:], push[rows - near:]]),
        odd,
    )
    stiff = jnp.concatenate([low[:wide], stiff, high[:wide]])
    pull = jnp.concatenate([low[wide:wide + near], pull, high[wide:wide + near]])
    push = jnp.concatenate([low[wide + near:], push, high[wide + near:]])

    first = time_slot == 0
    edge = jnp.where(first, edge_own, edge_in)
    mid = jnp.where(first, mid_own, mid_in)
    low, high = exchanged(edge[:side], edge[side:2 * side], odd)
    inside = rows - 2 * far
    position = jnp.concatenate(
        [low[:far], edge[:far], mid[:inside], edge[side:side + far], high[:far]]
    )
    velocity = jnp.concatenate(
        [low[far:], edge[far:side], mid[inside:], edge[side + far:2 * side], high[far:]]
    )
    gusts = jnp.stack([edge[2 * side], edge_own[2 * side]])

    out = chain_call(
        time_slot.reshape(1), position, velocity, stiff, pull, push, gusts, rows, far
    )
    return from_tile_view(out, start_state.shape)


def layered_device(*args):
    return two_slice_device(*args)


def chosen_device(start_state, rigidity, inv_mass, gust_load, kl_coeff, gust_history):
    rows, cols = rigidity.shape
    fits = cols == SUBLANES * LANES and rows % SUBLANES == 0 and rows > 4 * (2 * FINE + 1)
    two_slices = lax.axis_size("tm") == 2 and ITERS == 2 and start_state.shape[0] == 1
    device = layered_device if fits and two_slices else per_device
    return device(start_state, rigidity, inv_mass, gust_load, kl_coeff, gust_history)


def solution(mesh):
    in_specs = (
        P("tm", None, "space", None),
        P("space", None),
        P("space", None),
        P("space", None),
        P(),
        P("tm"),
    )
    out_specs = P("tm", None, "space", None)
    return jax.shard_map(
        chosen_device, mesh=mesh, in_specs=in_specs, out_specs=out_specs, check_vma=False
    )
```

```python
import functools

import jax
import jax.numpy as jnp
from jax import lax
from jax.experimental import pallas as pl
from jax.experimental.pallas import tpu as pltpu
from jax.sharding import PartitionSpec as P


FINE = 4
ITERS = 2
KL = 4


STIFF_SCALE = 1.0 / 64.0
TIME_STEP = 0.18
HALF_STEP = 0.09
DAMPING = 0.05


def extended(block, sides, width):
    for axis, dim in sides:
        count = lax.axis_size(axis)
        forward = [(i, i + 1) for i in range(count - 1)]
        backward = [(target, source) for source, target in forward]
        low = lax.ppermute(
            lax.slice_in_dim(block, block.shape[dim] - width, None, axis=dim), axis, forward
        )
        high = lax.ppermute(lax.slice_in_dim(block, 0, width, axis=dim), axis, backward)
        block = jnp.concatenate([low, block, high], axis=dim)
    return block


def passed_along(block, axis, distance):
    devices = range(lax.axis_size(axis))
    route = [(i - distance, i) for i in devices if i - distance in devices]
    return lax.ppermute(block, axis, route)


def laplace(padded):
    return (
        padded[2:, 1:-1]
        + padded[:-2, 1:-1]
        + padded[1:-1, 2:]
        + padded[1:-1, :-2]
        - 4.0 * padded[1:-1, 1:-1]
    )


def mode_table(positions, extent):
    orders = (jnp.arange(KL) + 1).astype(jnp.float32)
    coords = (positions.astype(jnp.float32) + 0.5) / extent
    return jnp.cos(jnp.pi * orders[:, None] * coords[None, :])


def build_rigidity(rigidity, kl_coeff, first_row, extent_rows, extent_cols):
    row_count = rigidity.shape[0]
    col_count = rigidity.shape[1]
    across = mode_table(first_row + jnp.arange(row_count), extent_rows)
    along_chord = mode_table(jnp.arange(col_count), extent_cols)
    mixed = jnp.dot(kl_coeff, along_chord, precision=lax.Precision.HIGHEST)
    kl_field = jnp.dot(across.T, mixed, precision=lax.Precision.HIGHEST)
    return rigidity * jnp.exp(0.5 * jnp.tanh(kl_field))


def apply_padded(widened, rigid_rim):
    weighted = rigid_rim * laplace(jnp.pad(widened, ((0, 0), (1, 1))))
    return STIFF_SCALE * laplace(jnp.pad(weighted, ((0, 0), (1, 1))))


def crop_rows(values_in, have_rim, want_rim):
    margin = have_rim - want_rim
    return values_in[margin : values_in.shape[0] - margin]


def accelerate(velocity, stiff_now, inv_mass, gust_load, gust_value):
    return inv_mass * (gust_load * gust_value - stiff_now) - DAMPING * velocity


def coarse_step(position, velocity, stiff_now, inv_mass, gust_load, gust_value):
    coarse_span = FINE * TIME_STEP
    new_vel = velocity + coarse_span * accelerate(
        velocity, stiff_now, inv_mass, gust_load, gust_value
    )
    return (position + coarse_span * new_vel, new_vel)


def per_device(start_state, rigidity, inv_mass, gust_load, kl_coeff, gust_history):
    row_count = rigidity.shape[0]
    col_count = rigidity.shape[1]
    space_count = lax.axis_size("space")
    time_count = lax.axis_size("tm")
    time_slot = lax.axis_index("tm")
    space_slot = lax.axis_index("space")
    stiff_field = build_rigidity(
        rigidity, kl_coeff, space_slot * row_count, row_count * space_count, col_count
    )
    reach = 2 * (FINE + 1)
    statics = extended(jnp.stack([stiff_field, inv_mass, gust_load]), (("space", 1),), reach)
    rigid_wide = statics[0]
    mass_wide = statics[1]
    load_wide = statics[2]
    rigid_one = crop_rows(rigid_wide, reach, 1)

    def coarse_stiff(moved):
        widened = extended(moved, (("space", 0),), 2)
        return apply_padded(widened, rigid_one)

    def coarse_move(position, velocity, stiff_now, gust_value):
        return coarse_step(position, velocity, stiff_now, inv_mass, gust_load, gust_value)

    position = start_state[0, 0]
    velocity = start_state[0, 1]
    end_pos = position
    end_vel = velocity
    for sweep_index in range(ITERS):
        last_sweep = sweep_index == ITERS - 1
        both = extended(jnp.stack([position, velocity]), (("space", 1),), reach)
        rim_now = reach
        fine_stiff_now = apply_padded(both[0], crop_rows(rigid_wide, reach, rim_now - 1))
        next_rim = rim_now - 2
        first_stiff = crop_rows(fine_stiff_now, next_rim, 0)
        pos_now = crop_rows(both[0], rim_now, next_rim)
        vel_now = crop_rows(both[1], rim_now, next_rim)
        rim_now = next_rim
        for step_index in range(FINE):
            fine_gust_value = gust_history[step_index]
            mass_now = crop_rows(mass_wide, reach, rim_now)
            load_now = crop_rows(load_wide, reach, rim_now)
            half_vel = vel_now + HALF_STEP * accelerate(
                vel_now, fine_stiff_now, mass_now, load_now, fine_gust_value
            )
            pos_now = pos_now + TIME_STEP * half_vel
            fine_stiff_now = apply_padded(pos_now, crop_rows(rigid_wide, reach, rim_now - 1))
            next_rim = rim_now - 2
            pos_now = crop_rows(pos_now, rim_now, next_rim)
            half_vel = crop_rows(half_vel, rim_now, next_rim)
            mass_now = crop_rows(mass_wide, reach, next_rim)
            load_now = crop_rows(load_wide, reach, next_rim)
            vel_now = half_vel + HALF_STEP * accelerate(
                half_vel, fine_stiff_now, mass_now, load_now, fine_gust_value
            )
            rim_now = next_rim
        fine_pos, fine_vel, first_stiff = (pos_now, vel_now, first_stiff)
        coarse_pos, coarse_vel = coarse_move(position, velocity, first_stiff, gust_history[0])
        delta_pos = fine_pos - coarse_pos
        delta_vel = fine_vel - coarse_vel
        chain_pos = position
        chain_vel = velocity
        for turn_index in range(1, time_count):
            stiff_now = coarse_stiff(chain_pos)
            moved_pos, moved_vel = coarse_move(chain_pos, chain_vel, stiff_now, gust_history[0])
            outgoing = jnp.stack([moved_pos + delta_pos, moved_vel + delta_vel])
            arrived = passed_along(outgoing, "tm", 1)
            chain_pos = jnp.where(time_slot == turn_index, arrived[0], chain_pos)
            chain_vel = jnp.where(time_slot == turn_index, arrived[1], chain_vel)
        if last_sweep:
            stiff_now = coarse_stiff(chain_pos)
            moved_pos, moved_vel = coarse_move(chain_pos, chain_vel, stiff_now, gust_history[0])
            end_pos = moved_pos + delta_pos
            end_vel = moved_vel + delta_vel
        position = chain_pos
        velocity = chain_vel
    return jnp.stack([end_pos, end_vel])[None]


LANES = 128
SUBLANES = 8
COARSE_SPAN = FINE * TIME_STEP
DECAY = 1.0 - HALF_STEP * DAMPING
COARSE_DECAY = 1.0 - COARSE_SPAN * DAMPING
KICK = TIME_STEP * HALF_STEP
UNROLL = 32


def tile_view(block):
    width = block.shape[-1] // LANES
    tiles = block.reshape(-1, SUBLANES, width, LANES).transpose(0, 2, 1, 3)
    return tiles.reshape(-1, LANES)


def from_tile_view(view, shape):
    width = shape[-1] // LANES
    tiles = view.reshape(-1, width, SUBLANES, LANES).transpose(0, 2, 1, 3)
    return tiles.reshape(shape)


def row_at(view_ref, group, row):
    start = pl.multiple_of(group * SUBLANES * SUBLANES, SUBLANES * SUBLANES)
    return view_ref[pl.ds(start + row, SUBLANES, stride=SUBLANES), :]


def pack_kernel(
    gust_hbm, view_hbm, edge_ref, mid_ref, view_ref, gust_ref, sems, *, rows, far, near
):
    gust_copy = pltpu.make_async_copy(gust_hbm, gust_ref, sems.at[2])
    half = rows * SUBLANES
    copies = []
    for part in range(2):
        piece = pl.ds(part * half, half)
        copies.append(
            pltpu.make_async_copy(view_hbm.at[piece], view_ref.at[piece], sems.at[part])
        )
        copies[part].start()
    gust_copy.start()
    side = far + near
    for part, width, at in ((0, far, 0), (1, near, far)):
        copies[part].wait()
        for row in range(rows):
            group = (part * rows + row) // SUBLANES
            value = row_at(view_ref, group, row % SUBLANES)
            if row < width:
                edge_ref[at + row] = value
            elif row >= rows - width:
                edge_ref[side + at + row - (rows - width)] = value
            else:
                mid_ref[part * (rows - 2 * far) + row - width] = value
    gust_copy.wait()
    sub = lax.broadcasted_iota(jnp.int32, (SUBLANES, LANES), 0)
    gusts = jnp.zeros((SUBLANES, LANES), jnp.float32)
    for step_index in range(FINE):
        gusts = jnp.where(sub == step_index, gust_ref[step_index], gusts)
    edge_ref[2 * side] = gusts


def field_kernel(
    across_ref, along_ref, kl_hbm, rigid_hbm, mass_hbm, load_hbm, stiff_ref, pull_ref, push_ref,
    kl_ref, rigid_ref, mass_ref, load_ref, sems
):
    copies = [
        pltpu.make_async_copy(source, target, sems.at[at])
        for at, (source, target) in enumerate(
            (
                (kl_hbm, kl_ref),
                (rigid_hbm, rigid_ref),
                (mass_hbm, mass_ref),
                (load_hbm, load_ref),
            )
        )
    ]
    for copy in copies:
        copy.start()
    for copy in copies:
        copy.wait()
    rows = stiff_ref.shape[0]
    mixed = []
    for order in range(KL):
        total = kl_ref[order, 0] * along_ref[0]
        for other in range(1, KL):
            total = total + kl_ref[order, other] * along_ref[other]
        mixed.append(total)

    def group_rows(group, carry):
        for row in range(SUBLANES):
            at = group * SUBLANES + row
            field = across_ref[0, at] * mixed[0]
            for order in range(1, KL):
                field = field + across_ref[order, at] * mixed[order]
            mass = row_at(mass_ref, group, row)
            stiff_ref[at] = row_at(rigid_ref, group, row) * jnp.exp(0.5 * jnp.tanh(field))
            pull_ref[at] = (KICK * (1.0 + DECAY) * STIFF_SCALE) * mass
            push_ref[at] = KICK * (mass * row_at(load_ref, group, row))
        return carry

    lax.fori_loop(0, rows // SUBLANES, group_rows, 0)


def beside(row):
    lane = lax.broadcasted_iota(jnp.int32, (SUBLANES, LANES), 1)
    sub = lax.broadcasted_iota(jnp.int32, (SUBLANES, LANES), 0)
    last_lane = lane == LANES - 1
    first_lane = lane == 0
    below = jnp.where(last_lane, pltpu.roll(row, 1, 0), row)
    above = jnp.where(first_lane, pltpu.roll(row, SUBLANES - 1, 0), row)
    below = jnp.where(last_lane & (sub == 0), 0.0, below)
    above = jnp.where(first_lane & (sub == SUBLANES - 1), 0.0, above)
    return pltpu.roll(below, 1, 1) + pltpu.roll(above, LANES - 1, 1)


def splat(value):
    return jnp.full((SUBLANES, LANES), value, jnp.float32)


def gust_row(gust_ref, step_index):
    stage, at = divmod(step_index, FINE)
    return jnp.broadcast_to(gust_ref[stage, at:at + 1, :], (SUBLANES, LANES))


HALF_PULL = 1.0 / (1.0 + DECAY)


def fill_coef(coef, gust_ref, slot):
    for index in range(2 * FINE + 1):
        if index == 0:
            terms = splat(DECAY * TIME_STEP), gust_row(gust_ref, 0), splat(HALF_PULL)
        elif index == 2 * FINE:
            terms = (
                splat(DECAY / TIME_STEP),
                gust_row(gust_ref, index - 1) / TIME_STEP,
                splat(HALF_PULL / TIME_STEP),
            )
        else:
            both = DECAY * gust_row(gust_ref, index - 1) + gust_row(gust_ref, index)
            terms = splat(DECAY * DECAY), both, splat(1.0)
        for at, term in enumerate(terms):
            coef[index, at] = term

    @pl.when(slot == 0)
    def _():
        coef[FINE, 0] = splat(DECAY / TIME_STEP)
        coef[FINE, 1] = gust_row(gust_ref, FINE - 1) / TIME_STEP
        coef[FINE, 2] = splat(HALF_PULL / TIME_STEP)


def advance_rows(sweep, start, count, offset, pos, vel, coef, stiff_ref, pull_ref, push_ref):
    here = [pos[sweep, start - 2 + i] for i in range(count + 4)]
    sides = [beside(here[i]) for i in range(1, count + 3)]
    weighted = [
        stiff_ref[start - 1 + i - offset]
        * (here[i] + here[i + 2] + sides[i] - 4.0 * here[i + 1])
        for i in range(count + 2)
    ]
    alpha, push_by, pull_by = (coef[sweep, i] for i in range(3))
    moved = []
    for i in range(count):
        row = start + i
        bent = weighted[i] + weighted[i + 2] + beside(weighted[i + 1]) - 4.0 * weighted[i + 1]
        shift = (
            alpha * vel[sweep, row]
            + push_by * push_ref[row - offset]
            - pull_by * (pull_ref[row - offset] * bent)
        )
        moved.append((row, here[i + 2] + shift, shift))
    return moved


def keep_rows(sweep, moved, pos, vel):
    for row, position, shift in moved:
        pos[sweep + 1, row] = position
        vel[sweep + 1, row] = shift


def inner_kernel(
    slot_ref, edge_ref, mid_ref, stiff_ref, pull_ref, push_ref, gust_ref, pos, vel, coef,
    *, rows, far
):
    near = far - 2
    side = far + near
    top = far + 2
    slot = slot_ref[0]
    fill_coef(coef, gust_ref, slot)
    inside = rows - 2 * far
    for plane_ref, width, at, first in ((pos, far, 0, 0), (vel, near, far, inside)):
        for i in range(width):
            plane_ref[0, top + i] = edge_ref[at + i]
            plane_ref[0, top + rows - width + i] = edge_ref[side + at + i]
        for i in range(rows - 2 * width):
            plane_ref[0, top + width + i] = mid_ref[first + i]

    def sweep_all(sweep, carry):
        first = 2 * sweep + 2
        end = rows - first

        def chunk(index, carry):
            start = jnp.minimum(first + index * UNROLL, end - UNROLL) + top
            moved = advance_rows(
                sweep, start, UNROLL, top, pos, vel, coef, stiff_ref, pull_ref, push_ref
            )
            keep_rows(sweep, moved, pos, vel)
            return carry

        return lax.fori_loop(0, (end - first + UNROLL - 1) // UNROLL, chunk, carry)

    lax.fori_loop(0, jnp.where(slot == 0, FINE + 1, 2 * FINE + 1), sweep_all, 0)


def outer_kernel(
    slot_ref, odd_ref, inner_halo, outer_halo, stiff_ref, pull_ref, push_ref, gust_ref, pos_in,
    vel_in, pos, vel, out_ref, coef, *, rows, far
):
    near = far - 2
    top = far + 2
    slot = slot_ref[0]
    sweeps = jnp.where(slot == 0, FINE + 1, 2 * FINE + 1)
    fill_coef(coef, gust_ref, slot)

    def fill_halo(low, high):
        for i in range(far):
            pos[0, top - far + i] = low[i]
            pos[0, top + rows + i] = high[i]
        for i in range(near):
            vel[0, top - near + i] = low[far + i]
            vel[0, top + rows + i] = high[far + i]

    @pl.when(odd_ref[0] == 0)
    def _():
        fill_halo(outer_halo, inner_halo)

    @pl.when(odd_ref[0] != 0)
    def _():
        fill_halo(inner_halo, outer_halo)

    def sweep_all(sweep, carry):
        moved = []
        for start in (top - near + 2 * sweep, top + rows - 2 - 2 * sweep):
            moved += advance_rows(
                sweep, start, far, 0, pos, vel, coef, stiff_ref, pull_ref, push_ref
            )
        keep_rows(sweep, moved, pos, vel)
        return carry

    lax.fori_loop(0, sweeps, sweep_all, 0)

    begin = slot * FINE
    own = slot == 0
    by_start = splat(jnp.where(own, TIME_STEP, DECAY * HALF_PULL))
    by_next = splat(jnp.where(own, 0.0, HALF_PULL))
    gust_step = gust_row(gust_ref, FINE - 1) - gust_row(gust_ref, FINE)
    by_push = jnp.where(own, 0.0, HALF_PULL) * gust_step

    def finish(group, carry):
        first = pl.multiple_of(group * SUBLANES * SUBLANES, SUBLANES * SUBLANES)
        for j in range(SUBLANES):
            row = group * SUBLANES + j + top
            following = vel[begin + 1, row]
            scaled = by_start * vel[begin, row] + by_next * following + by_push * push_ref[row]
            force = following - DECAY * scaled
            coarse_vel = (COARSE_DECAY / TIME_STEP) * scaled + (COARSE_SPAN / KICK) * force
            coarse_pos = pos[begin, row] + COARSE_SPAN * coarse_vel
            delta_pos = pos[sweeps - 1, row] - coarse_pos
            delta_vel = vel[sweeps, row] - coarse_vel
            at = first + j
            out_ref[pl.ds(at, SUBLANES, stride=SUBLANES), :] = coarse_pos + delta_pos
            out_ref[pl.ds(at + rows * SUBLANES, SUBLANES, stride=SUBLANES), :] = (
                coarse_vel + delta_vel
            )
        return carry

    lax.fori_loop(0, rows // SUBLANES, finish, 0)


def swap_pairs(count, first):
    pairs = [(i, i + 1) for i in range(first, count - 1, 2)]
    return pairs + [(target, source) for source, target in pairs]


def exchanged(low_rows, high_rows, odd):
    count = lax.axis_size("space")
    inner = lax.ppermute(jnp.where(odd, low_rows, high_rows), "space", swap_pairs(count, 0))
    outer = lax.ppermute(jnp.where(odd, high_rows, low_rows), "space", swap_pairs(count, 1))
    return inner, outer


def in_vmem(count):
    return [pl.BlockSpec(memory_space=pltpu.VMEM)] * count


def in_smem(count):
    return [pl.BlockSpec(memory_space=pltpu.SMEM)] * count


def in_hbm(array):
    return pltpu.with_memory_space_constraint(array, pltpu.HBM)


def plane(count):
    return jax.ShapeDtypeStruct((count, SUBLANES, LANES), jnp.float32)


def field_call(across, along, kl_coeff, rigidity, inv_mass, gust_load):
    rows = rigidity.shape[0] // SUBLANES
    return pl.pallas_call(
        field_kernel,
        out_shape=(plane(rows),) * 3,
        in_specs=in_smem(1) + in_vmem(1) + [pl.BlockSpec(memory_space=pltpu.HBM)] * 4,
        out_specs=tuple(in_vmem(3)),
        scratch_shapes=[pltpu.SMEM((KL, KL), jnp.float32)]
        + [pltpu.VMEM(rigidity.shape, jnp.float32)] * 3
        + [pltpu.SemaphoreType.DMA((4,))],
        compiler_params=pltpu.CompilerParams(vmem_limit_bytes=16 * 2**20),
        name="field",
    )(
        across,
        along,
        in_hbm(kl_coeff),
        in_hbm(rigidity),
        in_hbm(inv_mass),
        in_hbm(gust_load),
    )


def state_planes(rows, far):
    shape = (2 * FINE + 2, rows + 2 * far + 4, SUBLANES, LANES)
    return jax.ShapeDtypeStruct(shape, jnp.float32)


def coef_scratch():
    return [pltpu.VMEM((2 * FINE + 1, 3, SUBLANES, LANES), jnp.float32)]


def inner_call(slot, edge, mid, stiff, pull, push, gusts, rows, far):
    return pl.pallas_call(
        functools.partial(inner_kernel, rows=rows, far=far),
        out_shape=(state_planes(rows, far),) * 2,
        in_specs=in_smem(1) + in_vmem(6),
        out_specs=tuple(in_vmem(2)),
        scratch_shapes=coef_scratch(),
        compiler_params=pltpu.CompilerParams(vmem_limit_bytes=24 * 2**20),
        name="inner",
    )(slot, edge, mid, stiff, pull, push, gusts)


def outer_call(slot, odd, inner, outer, stiff, pull, push, gusts, pos, vel, rows, far):
    planes = state_planes(rows, far)
    out = jax.ShapeDtypeStruct((2 * rows * SUBLANES, LANES), jnp.float32)
    return pl.pallas_call(
        functools.partial(outer_kernel, rows=rows, far=far),
        out_shape=(planes, planes, out),
        in_specs=in_smem(2) + in_vmem(8),
        out_specs=tuple(in_vmem(3)),
        scratch_shapes=coef_scratch(),
        input_output_aliases={8: 0, 9: 1},
        compiler_params=pltpu.CompilerParams(vmem_limit_bytes=24 * 2**20),
        name="outer",
    )(slot, odd, inner, outer, stiff, pull, push, gusts, pos, vel)[2]


def two_slice_device(start_state, rigidity, inv_mass, gust_load, kl_coeff, gust_history):
    rows, cols = rigidity.shape
    far = 2 * (2 * FINE + 1)
    near = far - 2
    side = far + near
    time_slot = lax.axis_index("tm")
    space_slot = lax.axis_index("space")
    odd = space_slot % 2 == 1
    small = pltpu.CompilerParams(vmem_limit_bytes=16 * 2**20)

    edge_own, mid_own = pl.pallas_call(
        functools.partial(pack_kernel, rows=rows, far=far, near=near),
        out_shape=(plane(2 * side + 1), plane(2 * rows - 2 * side)),
        in_specs=[pl.BlockSpec(memory_space=pltpu.HBM)] * 2,
        out_specs=tuple(in_vmem(2)),
        scratch_shapes=[
            pltpu.VMEM((2 * rows * SUBLANES, LANES), jnp.float32),
            pltpu.SMEM((FINE,), jnp.float32),
            pltpu.SemaphoreType.DMA((3,)),
        ],
        compiler_params=small,
        name="pack",
    )(in_hbm(gust_history), in_hbm(tile_view(start_state)))
    edge_in = passed_along(edge_own, "tm", 1)
    mid_in = passed_along(mid_own, "tm", 1)
    edge_own, rigidity, inv_mass, gust_load = lax.optimization_barrier(
        (edge_own, rigidity, inv_mass, gust_load)
    )

    across = mode_table(space_slot * rows + jnp.arange(rows), rows * lax.axis_size("space"))
    along = mode_table(jnp.arange(cols), cols).reshape(KL, SUBLANES, LANES)
    stiff, pull, push = field_call(
        across, along, kl_coeff, tile_view(rigidity), tile_view(inv_mass), tile_view(gust_load)
    )
    wide = far - 1
    still_inner, still_outer = exchanged(
        jnp.concatenate([stiff[:wide], pull[:near], push[:near]]),
        jnp.concatenate([stiff[rows - wide:], pull[rows - near:], push[rows - near:]]),
        odd,
    )

    first = time_slot == 0
    edge = jnp.where(first, edge_own, edge_in)
    mid = jnp.where(first, mid_own, mid_in)
    inner, outer = exchanged(edge[:side], edge[side:2 * side], odd)
    gusts = jnp.stack([edge[2 * side], edge_own[2 * side]])
    slot = time_slot.reshape(1)
    pos, vel = inner_call(slot, edge, mid, stiff, pull, push, gusts, rows, far)

    low = jnp.where(odd, still_inner, still_outer)
    high = jnp.where(odd, still_outer, still_inner)

    def spread(low_rows, own_rows, high_rows):
        margin = far + 2 - low_rows.shape[0]
        block = jnp.concatenate([low_rows, own_rows, high_rows])
        return jnp.pad(block, ((margin, margin), (0, 0), (0, 0)))

    stiff = spread(low[:wide], stiff, high[:wide])
    pull = spread(low[wide:wide + near], pull, high[wide:wide + near])
    push = spread(low[wide + near:], push, high[wide + near:])
    parity = odd.astype(jnp.int32).reshape(1)
    out = outer_call(
        slot, parity, inner, outer, stiff, pull, push, gusts, pos, vel, rows, far
    )
    return from_tile_view(out, start_state.shape)


def layered_device(*args):
    return two_slice_device(*args)


def chosen_device(start_state, rigidity, inv_mass, gust_load, kl_coeff, gust_history):
    rows, cols = rigidity.shape
    fits = cols == SUBLANES * LANES and rows % SUBLANES == 0 and rows >= 2 * UNROLL
    two_slices = lax.axis_size("tm") == 2 and ITERS == 2 and start_state.shape[0] == 1
    device = layered_device if fits and two_slices else per_device
    return device(start_state, rigidity, inv_mass, gust_load, kl_coeff, gust_history)


def solution(mesh):
    in_specs = (
        P("tm", None, "space", None),
        P("space", None),
        P("space", None),
        P("space", None),
        P(),
        P("tm"),
    )
    out_specs = P("tm", None, "space", None)
    return jax.shard_map(
        chosen_device, mesh=mesh, in_specs=in_specs, out_specs=out_specs, check_vma=False
    )
```

```python
import functools

import jax
import jax.numpy as jnp
from jax import lax
from jax.experimental import pallas as pl
from jax.experimental.pallas import tpu as pltpu
from jax.sharding import PartitionSpec as P


FINE = 4
ITERS = 2
KL = 4


STIFF_SCALE = 1.0 / 64.0
TIME_STEP = 0.18
HALF_STEP = 0.09
DAMPING = 0.05


def extended(block, sides, width):
    for axis, dim in sides:
        count = lax.axis_size(axis)
        forward = [(i, i + 1) for i in range(count - 1)]
        backward = [(target, source) for source, target in forward]
        low = lax.ppermute(
            lax.slice_in_dim(block, block.shape[dim] - width, None, axis=dim), axis, forward
        )
        high = lax.ppermute(lax.slice_in_dim(block, 0, width, axis=dim), axis, backward)
        block = jnp.concatenate([low, block, high], axis=dim)
    return block


def passed_along(block, axis, distance):
    devices = range(lax.axis_size(axis))
    route = [(i - distance, i) for i in devices if i - distance in devices]
    return lax.ppermute(block, axis, route)


def laplace(padded):
    return (
        padded[2:, 1:-1]
        + padded[:-2, 1:-1]
        + padded[1:-1, 2:]
        + padded[1:-1, :-2]
        - 4.0 * padded[1:-1, 1:-1]
    )


def mode_table(positions, extent):
    orders = (jnp.arange(KL) + 1).astype(jnp.float32)
    coords = (positions.astype(jnp.float32) + 0.5) / extent
    return jnp.cos(jnp.pi * orders[:, None] * coords[None, :])


def build_rigidity(rigidity, kl_coeff, first_row, extent_rows, extent_cols):
    row_count = rigidity.shape[0]
    col_count = rigidity.shape[1]
    across = mode_table(first_row + jnp.arange(row_count), extent_rows)
    along_chord = mode_table(jnp.arange(col_count), extent_cols)
    mixed = jnp.dot(kl_coeff, along_chord, precision=lax.Precision.HIGHEST)
    kl_field = jnp.dot(across.T, mixed, precision=lax.Precision.HIGHEST)
    return rigidity * jnp.exp(0.5 * jnp.tanh(kl_field))


def apply_padded(widened, rigid_rim):
    weighted = rigid_rim * laplace(jnp.pad(widened, ((0, 0), (1, 1))))
    return STIFF_SCALE * laplace(jnp.pad(weighted, ((0, 0), (1, 1))))


def crop_rows(values_in, have_rim, want_rim):
    margin = have_rim - want_rim
    return values_in[margin : values_in.shape[0] - margin]


def accelerate(velocity, stiff_now, inv_mass, gust_load, gust_value):
    return inv_mass * (gust_load * gust_value - stiff_now) - DAMPING * velocity


def coarse_step(position, velocity, stiff_now, inv_mass, gust_load, gust_value):
    coarse_span = FINE * TIME_STEP
    new_vel = velocity + coarse_span * accelerate(
        velocity, stiff_now, inv_mass, gust_load, gust_value
    )
    return (position + coarse_span * new_vel, new_vel)


def per_device(start_state, rigidity, inv_mass, gust_load, kl_coeff, gust_history):
    row_count = rigidity.shape[0]
    col_count = rigidity.shape[1]
    space_count = lax.axis_size("space")
    time_count = lax.axis_size("tm")
    time_slot = lax.axis_index("tm")
    space_slot = lax.axis_index("space")
    stiff_field = build_rigidity(
        rigidity, kl_coeff, space_slot * row_count, row_count * space_count, col_count
    )
    reach = 2 * (FINE + 1)
    statics = extended(jnp.stack([stiff_field, inv_mass, gust_load]), (("space", 1),), reach)
    rigid_wide = statics[0]
    mass_wide = statics[1]
    load_wide = statics[2]
    rigid_one = crop_rows(rigid_wide, reach, 1)

    def coarse_stiff(moved):
        widened = extended(moved, (("space", 0),), 2)
        return apply_padded(widened, rigid_one)

    def coarse_move(position, velocity, stiff_now, gust_value):
        return coarse_step(position, velocity, stiff_now, inv_mass, gust_load, gust_value)

    position = start_state[0, 0]
    velocity = start_state[0, 1]
    end_pos = position
    end_vel = velocity
    for sweep_index in range(ITERS):
        last_sweep = sweep_index == ITERS - 1
        both = extended(jnp.stack([position, velocity]), (("space", 1),), reach)
        rim_now = reach
        fine_stiff_now = apply_padded(both[0], crop_rows(rigid_wide, reach, rim_now - 1))
        next_rim = rim_now - 2
        first_stiff = crop_rows(fine_stiff_now, next_rim, 0)
        pos_now = crop_rows(both[0], rim_now, next_rim)
        vel_now = crop_rows(both[1], rim_now, next_rim)
        rim_now = next_rim
        for step_index in range(FINE):
            fine_gust_value = gust_history[step_index]
            mass_now = crop_rows(mass_wide, reach, rim_now)
            load_now = crop_rows(load_wide, reach, rim_now)
            half_vel = vel_now + HALF_STEP * accelerate(
                vel_now, fine_stiff_now, mass_now, load_now, fine_gust_value
            )
            pos_now = pos_now + TIME_STEP * half_vel
            fine_stiff_now = apply_padded(pos_now, crop_rows(rigid_wide, reach, rim_now - 1))
            next_rim = rim_now - 2
            pos_now = crop_rows(pos_now, rim_now, next_rim)
            half_vel = crop_rows(half_vel, rim_now, next_rim)
            mass_now = crop_rows(mass_wide, reach, next_rim)
            load_now = crop_rows(load_wide, reach, next_rim)
            vel_now = half_vel + HALF_STEP * accelerate(
                half_vel, fine_stiff_now, mass_now, load_now, fine_gust_value
            )
            rim_now = next_rim
        fine_pos, fine_vel, first_stiff = (pos_now, vel_now, first_stiff)
        coarse_pos, coarse_vel = coarse_move(position, velocity, first_stiff, gust_history[0])
        delta_pos = fine_pos - coarse_pos
        delta_vel = fine_vel - coarse_vel
        chain_pos = position
        chain_vel = velocity
        for turn_index in range(1, time_count):
            stiff_now = coarse_stiff(chain_pos)
            moved_pos, moved_vel = coarse_move(chain_pos, chain_vel, stiff_now, gust_history[0])
            outgoing = jnp.stack([moved_pos + delta_pos, moved_vel + delta_vel])
            arrived = passed_along(outgoing, "tm", 1)
            chain_pos = jnp.where(time_slot == turn_index, arrived[0], chain_pos)
            chain_vel = jnp.where(time_slot == turn_index, arrived[1], chain_vel)
        if last_sweep:
            stiff_now = coarse_stiff(chain_pos)
            moved_pos, moved_vel = coarse_move(chain_pos, chain_vel, stiff_now, gust_history[0])
            end_pos = moved_pos + delta_pos
            end_vel = moved_vel + delta_vel
        position = chain_pos
        velocity = chain_vel
    return jnp.stack([end_pos, end_vel])[None]


LANES = 128
SUBLANES = 8
COARSE_SPAN = FINE * TIME_STEP
DECAY = 1.0 - HALF_STEP * DAMPING
COARSE_DECAY = 1.0 - COARSE_SPAN * DAMPING
KICK = TIME_STEP * HALF_STEP
UNROLL = 60


def tile_view(block):
    width = block.shape[-1] // LANES
    tiles = block.reshape(-1, SUBLANES, width, LANES).transpose(0, 2, 1, 3)
    return tiles.reshape(-1, LANES)


def from_tile_view(view, shape):
    width = shape[-1] // LANES
    tiles = view.reshape(-1, width, SUBLANES, LANES).transpose(0, 2, 1, 3)
    return tiles.reshape(shape)


def row_at(view_ref, group, row):
    start = pl.multiple_of(group * SUBLANES * SUBLANES, SUBLANES * SUBLANES)
    return view_ref[pl.ds(start + row, SUBLANES, stride=SUBLANES), :]


def gusts_of(gust_ref):
    sub = lax.broadcasted_iota(jnp.int32, (SUBLANES, LANES), 0)
    gusts = jnp.zeros((SUBLANES, LANES), jnp.float32)
    for step_index in range(FINE):
        gusts = jnp.where(sub == step_index, gust_ref[step_index], gusts)
    return gusts


def pack_kernel(slot_ref, odd_ref, *refs, rows, far):
    @pl.when(slot_ref[0] == 0)
    def _():
        pack_rows(odd_ref, *refs, rows=rows, far=far)


def pack_rows(
    odd_ref, gust_hbm, view_hbm, first_ref, second_ref, mid_ref, view_ref, gust_ref, sems,
    *, rows, far
):
    gust_copy = pltpu.make_async_copy(gust_hbm, gust_ref, sems.at[2])
    half = rows * SUBLANES
    copies = []
    for part in range(2):
        piece = pl.ds(part * half, half)
        copies.append(
            pltpu.make_async_copy(view_hbm.at[piece], view_ref.at[piece], sems.at[part])
        )
        copies[part].start()
    gust_copy.start()
    near = far - 2
    parts = ((0, far, 0), (1, near, far))

    def state_row(part, row):
        return row_at(view_ref, (part * rows + row) // SUBLANES, row % SUBLANES)

    def edges(low_ref, high_ref):
        for part, width, at in parts:
            for i in range(width):
                low_ref[at + i] = state_row(part, i)
                high_ref[at + i] = state_row(part, rows - width + i)

    for part, width, at in parts:
        copies[part].wait()
        for row in range(width, rows - width):
            mid_ref[part * (rows - 2 * far) + row - width] = state_row(part, row)

    @pl.when(odd_ref[0] == 0)
    def _():
        edges(first_ref, second_ref)

    @pl.when(odd_ref[0] != 0)
    def _():
        edges(second_ref, first_ref)

    gust_copy.wait()
    first_ref[far + near] = gusts_of(gust_ref)


def field_kernel(
    across_ref, along_ref, kl_hbm, gust_hbm, rigid_hbm, mass_hbm, load_hbm, stiff_ref, pull_ref,
    push_ref, gust_out, kl_ref, gust_ref, rigid_ref, mass_ref, load_ref, sems
):
    copies = [
        pltpu.make_async_copy(source, target, sems.at[at])
        for at, (source, target) in enumerate(
            (
                (kl_hbm, kl_ref),
                (gust_hbm, gust_ref),
                (rigid_hbm, rigid_ref),
                (mass_hbm, mass_ref),
                (load_hbm, load_ref),
            )
        )
    ]
    for copy in copies:
        copy.start()
    for copy in copies[:2]:
        copy.wait()
    gust_out[...] = gusts_of(gust_ref)
    rows = stiff_ref.shape[0]
    mixed = []
    for order in range(KL):
        total = kl_ref[order, 0] * along_ref[0]
        for other in range(1, KL):
            total = total + kl_ref[order, other] * along_ref[other]
        mixed.append(total)

    def factor_rows(group, carry):
        for row in range(SUBLANES):
            at = group * SUBLANES + row
            field = across_ref[0, at] * mixed[0]
            for order in range(1, KL):
                field = field + across_ref[order, at] * mixed[order]
            stiff_ref[at] = jnp.exp(0.5 * jnp.tanh(field))
        return carry

    lax.fori_loop(0, rows // SUBLANES, factor_rows, 0)
    for copy in copies[2:]:
        copy.wait()

    def group_rows(group, carry):
        for row in range(SUBLANES):
            at = group * SUBLANES + row
            mass = row_at(mass_ref, group, row)
            stiff_ref[at] = row_at(rigid_ref, group, row) * stiff_ref[at]
            pull_ref[at] = (KICK * (1.0 + DECAY) * STIFF_SCALE) * mass
            push_ref[at] = KICK * (mass * row_at(load_ref, group, row))
        return carry

    lax.fori_loop(0, rows // SUBLANES, group_rows, 0)


def beside(row):
    lane = lax.broadcasted_iota(jnp.int32, (SUBLANES, LANES), 1)
    sub = lax.broadcasted_iota(jnp.int32, (SUBLANES, LANES), 0)
    last_lane = lane == LANES - 1
    first_lane = lane == 0
    ends = (last_lane & (sub == SUBLANES - 1)) | (first_lane & (sub == 0))
    within = jnp.where(ends, 0.0, row)
    below = jnp.where(last_lane, pltpu.roll(within, 1, 0), row)
    above = jnp.where(first_lane, pltpu.roll(within, SUBLANES - 1, 0), row)
    return pltpu.roll(below, 1, 1) + pltpu.roll(above, LANES - 1, 1)


def splat(value):
    return jnp.full((SUBLANES, LANES), value, jnp.float32)


def gust_row(gust_ref, step_index):
    stage, at = divmod(step_index, FINE)
    return jnp.broadcast_to(gust_ref[stage, at:at + 1, :], (SUBLANES, LANES))


HALF_PULL = 1.0 / (1.0 + DECAY)


def fill_coef(coef, gust_ref, slot):
    for index in range(2 * FINE + 1):
        if index == 0:
            terms = splat(DECAY * TIME_STEP), gust_row(gust_ref, 0), splat(HALF_PULL)
        elif index == 2 * FINE:
            terms = (
                splat(DECAY / TIME_STEP),
                gust_row(gust_ref, index - 1) / TIME_STEP,
                splat(HALF_PULL / TIME_STEP),
            )
        else:
            both = DECAY * gust_row(gust_ref, index - 1) + gust_row(gust_ref, index)
            terms = splat(DECAY * DECAY), both, splat(1.0)
        for at, term in enumerate(terms):
            coef[index, at] = term

    @pl.when(slot == 0)
    def _():
        coef[FINE, 0] = splat(DECAY / TIME_STEP)
        coef[FINE, 1] = gust_row(gust_ref, FINE - 1) / TIME_STEP
        coef[FINE, 2] = splat(HALF_PULL / TIME_STEP)


def advance_rows(sweep, starts, count, offset, pos, vel, coef, stiff_ref, pull_ref, push_ref):
    here = [[pos[sweep, start - 2 + i] for i in range(count + 4)] for start in starts]
    sides = [[beside(rows[i]) for i in range(1, count + 3)] for rows in here]
    weighted = [
        [
            stiff_ref[start - 1 + i - offset]
            * (rows[i] + rows[i + 2] + side[i] - 4.0 * rows[i + 1])
            for i in range(count + 2)
        ]
        for start, rows, side in zip(starts, here, sides)
    ]
    weighted_sides = [[beside(row) for row in rows[1:-1]] for rows in weighted]
    alpha, push_by, pull_by = (coef[sweep, i] for i in range(3))
    moved = []
    for start, rows, heavy, side in zip(starts, here, weighted, weighted_sides):
        for i in range(count):
            row = start + i
            bent = heavy[i] + heavy[i + 2] + side[i] - 4.0 * heavy[i + 1]
            shift = (
                alpha * vel[sweep, row]
                + push_by * push_ref[row - offset]
                - pull_by * (pull_ref[row - offset] * bent)
            )
            moved.append((row, rows[i + 2] + shift, shift))
    return moved


def keep_rows(sweep, moved, pos, vel):
    for row, position, shift in moved:
        pos[sweep + 1, row] = position
        vel[sweep + 1, row] = shift


def inner_kernel(
    slot_ref, edge_ref, mid_ref, stiff_ref, pull_ref, push_ref, gust_ref, pos, vel, coef,
    *, rows, far
):
    near = far - 2
    side = far + near
    top = far + 2
    slot = slot_ref[0]
    fill_coef(coef, gust_ref, slot)
    inside = rows - 2 * far
    for plane_ref, width, at, first in ((pos, far, 0, 0), (vel, near, far, inside)):
        for i in range(width):
            plane_ref[0, top + i] = edge_ref[at + i]
            plane_ref[0, top + rows - width + i] = edge_ref[side + at + i]
        for i in range(rows - 2 * width):
            plane_ref[0, top + width + i] = mid_ref[first + i]

    def sweep_with(count):
        def sweep_all(sweep, carry):
            start = top + (rows - count) // 2
            moved = advance_rows(
                sweep, (start,), count, top, pos, vel, coef, stiff_ref, pull_ref, push_ref
            )
            keep_rows(sweep, moved, pos, vel)
            return carry

        return sweep_all

    early = 4
    sweeps = jnp.where(slot == 0, FINE + 1, 2 * FINE + 1)
    lax.fori_loop(0, early, sweep_with(rows - 4), 0)
    lax.fori_loop(early, sweeps, sweep_with(rows - 4 - 4 * early), 0)


def outer_kernel(
    slot_ref, odd_ref, inner_halo, outer_halo, stiff_ref, pull_ref, push_ref, gust_ref, pos_in,
    vel_in, pos, vel, out_ref, coef, *, rows, far
):
    near = far - 2
    top = far + 2
    slot = slot_ref[0]
    sweeps = jnp.where(slot == 0, FINE + 1, 2 * FINE + 1)
    fill_coef(coef, gust_ref, slot)

    def fill_halo(low, high):
        for i in range(far):
            pos[0, top - far + i] = low[i]
            pos[0, top + rows + i] = high[i]
        for i in range(near):
            vel[0, top - near + i] = low[far + i]
            vel[0, top + rows + i] = high[far + i]

    @pl.when(odd_ref[0] == 0)
    def _():
        fill_halo(outer_halo, inner_halo)

    @pl.when(odd_ref[0] != 0)
    def _():
        fill_halo(inner_halo, outer_halo)

    def sweep_all(sweep, carry):
        starts = (top - near + 2 * sweep, top + rows - 2 - 2 * sweep)
        moved = advance_rows(
            sweep, starts, far, 0, pos, vel, coef, stiff_ref, pull_ref, push_ref
        )
        keep_rows(sweep, moved, pos, vel)
        return carry

    lax.fori_loop(0, sweeps, sweep_all, 0)

    begin = slot * FINE
    own = slot == 0
    by_start = splat(jnp.where(own, TIME_STEP, DECAY * HALF_PULL))
    by_next = splat(jnp.where(own, 0.0, HALF_PULL))
    gust_step = gust_row(gust_ref, FINE - 1) - gust_row(gust_ref, FINE)
    by_push = jnp.where(own, 0.0, HALF_PULL) * gust_step

    def finish(group, carry):
        first = pl.multiple_of(group * SUBLANES * SUBLANES, SUBLANES * SUBLANES)
        for j in range(SUBLANES):
            row = group * SUBLANES + j + top
            following = vel[begin + 1, row]
            scaled = by_start * vel[begin, row] + by_next * following + by_push * push_ref[row]
            force = following - DECAY * scaled
            coarse_vel = (COARSE_DECAY / TIME_STEP) * scaled + (COARSE_SPAN / KICK) * force
            coarse_pos = pos[begin, row] + COARSE_SPAN * coarse_vel
            delta_pos = pos[sweeps - 1, row] - coarse_pos
            delta_vel = vel[sweeps, row] - coarse_vel
            at = first + j
            out_ref[pl.ds(at, SUBLANES, stride=SUBLANES), :] = coarse_pos + delta_pos
            out_ref[pl.ds(at + rows * SUBLANES, SUBLANES, stride=SUBLANES), :] = (
                coarse_vel + delta_vel
            )
        return carry

    lax.fori_loop(0, rows // SUBLANES, finish, 0)


def swap_pairs(count, first):
    pairs = [(i, i + 1) for i in range(first, count - 1, 2)]
    return pairs + [(target, source) for source, target in pairs]


def sent(block, pairs, within=None):
    if within is not None:
        base = within * lax.axis_size("space")
        pairs = [(base + source, base + target) for source, target in pairs]
    axes = "space" if within is None else ("tm", "space")
    return lax.ppermute(block, axes, pairs)


def in_vmem(count):
    return [pl.BlockSpec(memory_space=pltpu.VMEM)] * count


def in_smem(count):
    return [pl.BlockSpec(memory_space=pltpu.SMEM)] * count


def in_hbm(array):
    return pltpu.with_memory_space_constraint(array, pltpu.HBM)


def plane(count):
    return jax.ShapeDtypeStruct((count, SUBLANES, LANES), jnp.float32)


def field_call(across, along, kl_coeff, gust_history, rigidity, inv_mass, gust_load):
    rows = rigidity.shape[0] // SUBLANES
    return pl.pallas_call(
        field_kernel,
        out_shape=(plane(rows),) * 3 + (jax.ShapeDtypeStruct((SUBLANES, LANES), jnp.float32),),
        in_specs=in_smem(1) + in_vmem(1) + [pl.BlockSpec(memory_space=pltpu.HBM)] * 5,
        out_specs=tuple(in_vmem(4)),
        scratch_shapes=[
            pltpu.SMEM((KL, KL), jnp.float32),
            pltpu.SMEM((FINE,), jnp.float32),
        ]
        + [pltpu.VMEM(rigidity.shape, jnp.float32)] * 3
        + [pltpu.SemaphoreType.DMA((5,))],
        compiler_params=pltpu.CompilerParams(vmem_limit_bytes=16 * 2**20),
        name="field",
    )(
        across,
        along,
        in_hbm(kl_coeff),
        in_hbm(gust_history),
        in_hbm(rigidity),
        in_hbm(inv_mass),
        in_hbm(gust_load),
    )


def state_planes(rows, far):
    shape = (2 * FINE + 2, rows + 2 * far + 4, SUBLANES, LANES)
    return jax.ShapeDtypeStruct(shape, jnp.float32)


def coef_scratch():
    return [pltpu.VMEM((2 * FINE + 1, 3, SUBLANES, LANES), jnp.float32)]


def inner_call(slot, edge, mid, stiff, pull, push, gusts, rows, far):
    return pl.pallas_call(
        functools.partial(inner_kernel, rows=rows, far=far),
        out_shape=(state_planes(rows, far),) * 2,
        in_specs=in_smem(1) + in_vmem(6),
        out_specs=tuple(in_vmem(2)),
        scratch_shapes=coef_scratch(),
        compiler_params=pltpu.CompilerParams(vmem_limit_bytes=24 * 2**20),
        name="inner",
    )(slot, edge, mid, stiff, pull, push, gusts)


def outer_call(slot, odd, inner, outer, stiff, pull, push, gusts, pos, vel, rows, far):
    planes = state_planes(rows, far)
    out = jax.ShapeDtypeStruct((2 * rows * SUBLANES, LANES), jnp.float32)
    return pl.pallas_call(
        functools.partial(outer_kernel, rows=rows, far=far),
        out_shape=(planes, planes, out),
        in_specs=in_smem(2) + in_vmem(8),
        out_specs=tuple(in_vmem(3)),
        scratch_shapes=coef_scratch(),
        input_output_aliases={8: 0, 9: 1},
        compiler_params=pltpu.CompilerParams(vmem_limit_bytes=24 * 2**20),
        name="outer",
    )(slot, odd, inner, outer, stiff, pull, push, gusts, pos, vel)[2]


def two_slice_device(start_state, rigidity, inv_mass, gust_load, kl_coeff, gust_history):
    rows, cols = rigidity.shape
    far = 2 * (2 * FINE + 1)
    near = far - 2
    side = far + near
    time_slot = lax.axis_index("tm")
    space_slot = lax.axis_index("space")
    space_count = lax.axis_size("space")
    odd = space_slot % 2 == 1
    small = pltpu.CompilerParams(vmem_limit_bytes=16 * 2**20)

    slot = time_slot.reshape(1)
    parity = odd.astype(jnp.int32).reshape(1)
    first_own, second_own, mid_own = pl.pallas_call(
        functools.partial(pack_kernel, rows=rows, far=far),
        out_shape=(plane(side + 1), plane(side), plane(2 * rows - 2 * side)),
        in_specs=in_smem(2) + [pl.BlockSpec(memory_space=pltpu.HBM)] * 2,
        out_specs=tuple(in_vmem(3)),
        scratch_shapes=[
            pltpu.VMEM((2 * rows * SUBLANES, LANES), jnp.float32),
            pltpu.SMEM((FINE,), jnp.float32),
            pltpu.SemaphoreType.DMA((3,)),
        ],
        compiler_params=small,
        name="pack",
    )(slot, parity, in_hbm(gust_history), in_hbm(tile_view(start_state)))
    first_in = passed_along(first_own, "tm", 1)
    few = 2 * (FINE + 1)
    away = far - few
    early_rows = jnp.where(
        odd,
        jnp.concatenate([first_own[away:far], first_own[far + away:side]]),
        jnp.concatenate([first_own[:few], first_own[far:side - away]]),
    )
    early = sent(early_rows, swap_pairs(space_count, 1), 0)
    second_in = passed_along(second_own, "tm", 1)
    mid_in = passed_along(mid_own, "tm", 1)
    first_own, rigidity, inv_mass, gust_load = lax.optimization_barrier(
        (first_own, rigidity, inv_mass, gust_load)
    )

    across = mode_table(space_slot * rows + jnp.arange(rows), rows * lax.axis_size("space"))
    along = mode_table(jnp.arange(cols), cols).reshape(KL, SUBLANES, LANES)
    stiff, pull, push, own_gusts = field_call(
        across,
        along,
        kl_coeff,
        gust_history,
        tile_view(rigidity),
        tile_view(inv_mass),
        tile_view(gust_load),
    )
    wide = far - 1
    still_low = jnp.concatenate([stiff[:wide], pull[:near], push[:near]])
    still_high = jnp.concatenate(
        [stiff[rows - wide:], pull[rows - near:], push[rows - near:]]
    )
    still_outer = sent(jnp.where(odd, still_high, still_low), swap_pairs(space_count, 1))
    still_inner = sent(jnp.where(odd, still_low, still_high), swap_pairs(space_count, 0))

    own = time_slot == 0
    first_edge = jnp.where(own, first_own, first_in)
    mid = jnp.where(own, mid_own, mid_in)
    outer_late = sent(first_in, swap_pairs(space_count, 1), 1)
    second_edge = jnp.where(own, second_own, second_in)
    edge = jnp.concatenate(
        [
            jnp.where(odd, second_edge, first_edge[:side]),
            jnp.where(odd, first_edge[:side], second_edge),
        ]
    )
    inner = sent(second_edge, swap_pairs(space_count, 0))
    gusts = jnp.stack([first_edge[side], own_gusts])
    pos, vel = inner_call(slot, edge, mid, stiff, pull, push, gusts, rows, far)

    blank = jnp.zeros((away, SUBLANES, LANES), jnp.float32)
    of_even = jnp.concatenate([early[:few], blank, early[few:], blank])
    of_odd = jnp.concatenate([blank, early[:few], blank, early[few:]])
    outer = jnp.where(own, jnp.where(odd, of_even, of_odd), outer_late[:side])
    low = jnp.where(odd, still_inner, still_outer)
    high = jnp.where(odd, still_outer, still_inner)

    def spread(low_rows, own_rows, high_rows):
        margin = far + 2 - low_rows.shape[0]
        block = jnp.concatenate([low_rows, own_rows, high_rows])
        return jnp.pad(block, ((margin, margin), (0, 0), (0, 0)))

    stiff = spread(low[:wide], stiff, high[:wide])
    pull = spread(low[wide:wide + near], pull, high[wide:wide + near])
    push = spread(low[wide + near:], push, high[wide + near:])
    out = outer_call(
        slot, parity, inner, outer, stiff, pull, push, gusts, pos, vel, rows, far
    )
    return from_tile_view(out, start_state.shape)


def layered_device(*args):
    return two_slice_device(*args)


def chosen_device(start_state, rigidity, inv_mass, gust_load, kl_coeff, gust_history):
    rows, cols = rigidity.shape
    fits = cols == SUBLANES * LANES and rows % SUBLANES == 0 and rows >= UNROLL + 4
    two_slices = lax.axis_size("tm") == 2 and ITERS == 2 and start_state.shape[0] == 1
    device = layered_device if fits and two_slices else per_device
    return device(start_state, rigidity, inv_mass, gust_load, kl_coeff, gust_history)


def solution(mesh):
    in_specs = (
        P("tm", None, "space", None),
        P("space", None),
        P("space", None),
        P("space", None),
        P(),
        P("tm"),
    )
    out_specs = P("tm", None, "space", None)
    return jax.shard_map(
        chosen_device, mesh=mesh, in_specs=in_specs, out_specs=out_specs, check_vma=False
    )
```

```python
import functools

import jax
import jax.numpy as jnp
from jax import lax
from jax.experimental import pallas as pl
from jax.experimental.pallas import tpu as pltpu
from jax.sharding import PartitionSpec as P


FINE = 4
ITERS = 2
KL = 4


STIFF_SCALE = 1.0 / 64.0
TIME_STEP = 0.18
HALF_STEP = 0.09
DAMPING = 0.05


def extended(block, sides, width):
    for axis, dim in sides:
        count = lax.axis_size(axis)
        forward = [(i, i + 1) for i in range(count - 1)]
        backward = [(target, source) for source, target in forward]
        low = lax.ppermute(
            lax.slice_in_dim(block, block.shape[dim] - width, None, axis=dim), axis, forward
        )
        high = lax.ppermute(lax.slice_in_dim(block, 0, width, axis=dim), axis, backward)
        block = jnp.concatenate([low, block, high], axis=dim)
    return block


def passed_along(block, axis, distance):
    devices = range(lax.axis_size(axis))
    route = [(i - distance, i) for i in devices if i - distance in devices]
    return lax.ppermute(block, axis, route)


def laplace(padded):
    return (
        padded[2:, 1:-1]
        + padded[:-2, 1:-1]
        + padded[1:-1, 2:]
        + padded[1:-1, :-2]
        - 4.0 * padded[1:-1, 1:-1]
    )


def mode_table(positions, extent):
    orders = (jnp.arange(KL) + 1).astype(jnp.float32)
    coords = (positions.astype(jnp.float32) + 0.5) / extent
    return jnp.cos(jnp.pi * orders[:, None] * coords[None, :])


def build_rigidity(rigidity, kl_coeff, first_row, extent_rows, extent_cols):
    row_count = rigidity.shape[0]
    col_count = rigidity.shape[1]
    across = mode_table(first_row + jnp.arange(row_count), extent_rows)
    along_chord = mode_table(jnp.arange(col_count), extent_cols)
    mixed = jnp.dot(kl_coeff, along_chord, precision=lax.Precision.HIGHEST)
    kl_field = jnp.dot(across.T, mixed, precision=lax.Precision.HIGHEST)
    return rigidity * jnp.exp(0.5 * jnp.tanh(kl_field))


def apply_padded(widened, rigid_rim):
    weighted = rigid_rim * laplace(jnp.pad(widened, ((0, 0), (1, 1))))
    return STIFF_SCALE * laplace(jnp.pad(weighted, ((0, 0), (1, 1))))


def crop_rows(values_in, have_rim, want_rim):
    margin = have_rim - want_rim
    return values_in[margin : values_in.shape[0] - margin]


def accelerate(velocity, stiff_now, inv_mass, gust_load, gust_value):
    return inv_mass * (gust_load * gust_value - stiff_now) - DAMPING * velocity


def coarse_step(position, velocity, stiff_now, inv_mass, gust_load, gust_value):
    coarse_span = FINE * TIME_STEP
    new_vel = velocity + coarse_span * accelerate(
        velocity, stiff_now, inv_mass, gust_load, gust_value
    )
    return (position + coarse_span * new_vel, new_vel)


def per_device(start_state, rigidity, inv_mass, gust_load, kl_coeff, gust_history):
    row_count = rigidity.shape[0]
    col_count = rigidity.shape[1]
    space_count = lax.axis_size("space")
    time_count = lax.axis_size("tm")
    time_slot = lax.axis_index("tm")
    space_slot = lax.axis_index("space")
    stiff_field = build_rigidity(
        rigidity, kl_coeff, space_slot * row_count, row_count * space_count, col_count
    )
    reach = 2 * (FINE + 1)
    statics = extended(jnp.stack([stiff_field, inv_mass, gust_load]), (("space", 1),), reach)
    rigid_wide = statics[0]
    mass_wide = statics[1]
    load_wide = statics[2]
    rigid_one = crop_rows(rigid_wide, reach, 1)

    def coarse_stiff(moved):
        widened = extended(moved, (("space", 0),), 2)
        return apply_padded(widened, rigid_one)

    def coarse_move(position, velocity, stiff_now, gust_value):
        return coarse_step(position, velocity, stiff_now, inv_mass, gust_load, gust_value)

    position = start_state[0, 0]
    velocity = start_state[0, 1]
    end_pos = position
    end_vel = velocity
    for sweep_index in range(ITERS):
        last_sweep = sweep_index == ITERS - 1
        both = extended(jnp.stack([position, velocity]), (("space", 1),), reach)
        rim_now = reach
        fine_stiff_now = apply_padded(both[0], crop_rows(rigid_wide, reach, rim_now - 1))
        next_rim = rim_now - 2
        first_stiff = crop_rows(fine_stiff_now, next_rim, 0)
        pos_now = crop_rows(both[0], rim_now, next_rim)
        vel_now = crop_rows(both[1], rim_now, next_rim)
        rim_now = next_rim
        for step_index in range(FINE):
            fine_gust_value = gust_history[step_index]
            mass_now = crop_rows(mass_wide, reach, rim_now)
            load_now = crop_rows(load_wide, reach, rim_now)
            half_vel = vel_now + HALF_STEP * accelerate(
                vel_now, fine_stiff_now, mass_now, load_now, fine_gust_value
            )
            pos_now = pos_now + TIME_STEP * half_vel
            fine_stiff_now = apply_padded(pos_now, crop_rows(rigid_wide, reach, rim_now - 1))
            next_rim = rim_now - 2
            pos_now = crop_rows(pos_now, rim_now, next_rim)
            half_vel = crop_rows(half_vel, rim_now, next_rim)
            mass_now = crop_rows(mass_wide, reach, next_rim)
            load_now = crop_rows(load_wide, reach, next_rim)
            vel_now = half_vel + HALF_STEP * accelerate(
                half_vel, fine_stiff_now, mass_now, load_now, fine_gust_value
            )
            rim_now = next_rim
        fine_pos, fine_vel, first_stiff = (pos_now, vel_now, first_stiff)
        coarse_pos, coarse_vel = coarse_move(position, velocity, first_stiff, gust_history[0])
        delta_pos = fine_pos - coarse_pos
        delta_vel = fine_vel - coarse_vel
        chain_pos = position
        chain_vel = velocity
        for turn_index in range(1, time_count):
            stiff_now = coarse_stiff(chain_pos)
            moved_pos, moved_vel = coarse_move(chain_pos, chain_vel, stiff_now, gust_history[0])
            outgoing = jnp.stack([moved_pos + delta_pos, moved_vel + delta_vel])
            arrived = passed_along(outgoing, "tm", 1)
            chain_pos = jnp.where(time_slot == turn_index, arrived[0], chain_pos)
            chain_vel = jnp.where(time_slot == turn_index, arrived[1], chain_vel)
        if last_sweep:
            stiff_now = coarse_stiff(chain_pos)
            moved_pos, moved_vel = coarse_move(chain_pos, chain_vel, stiff_now, gust_history[0])
            end_pos = moved_pos + delta_pos
            end_vel = moved_vel + delta_vel
        position = chain_pos
        velocity = chain_vel
    return jnp.stack([end_pos, end_vel])[None]


LANES = 128
SUBLANES = 8
COARSE_SPAN = FINE * TIME_STEP
DECAY = 1.0 - HALF_STEP * DAMPING
COARSE_DECAY = 1.0 - COARSE_SPAN * DAMPING
KICK = TIME_STEP * HALF_STEP
UNROLL = 60


def tile_view(block):
    width = block.shape[-1] // LANES
    tiles = block.reshape(-1, SUBLANES, width, LANES).transpose(0, 2, 1, 3)
    return tiles.reshape(-1, LANES)


def from_tile_view(view, shape):
    width = shape[-1] // LANES
    tiles = view.reshape(-1, width, SUBLANES, LANES).transpose(0, 2, 1, 3)
    return tiles.reshape(shape)


def row_at(view_ref, group, row):
    start = pl.multiple_of(group * SUBLANES * SUBLANES, SUBLANES * SUBLANES)
    return view_ref[pl.ds(start + row, SUBLANES, stride=SUBLANES), :]


def gusts_of(gust_ref):
    sub = lax.broadcasted_iota(jnp.int32, (SUBLANES, LANES), 0)
    gusts = jnp.zeros((SUBLANES, LANES), jnp.float32)
    for step_index in range(FINE):
        gusts = jnp.where(sub == step_index, gust_ref[step_index], gusts)
    return gusts


def pack_kernel(slot_ref, odd_ref, *refs, rows, far):
    @pl.when(slot_ref[0] == 0)
    def _():
        pack_rows(odd_ref, *refs, rows=rows, far=far)


def pack_rows(
    odd_ref, gust_hbm, view_hbm, first_ref, second_ref, mid_ref, view_ref, gust_ref, sems,
    *, rows, far
):
    gust_copy = pltpu.make_async_copy(gust_hbm, gust_ref, sems.at[2])
    half = rows * SUBLANES
    copies = []
    for part in range(2):
        piece = pl.ds(part * half, half)
        copies.append(
            pltpu.make_async_copy(view_hbm.at[piece], view_ref.at[piece], sems.at[part])
        )
        copies[part].start()
    gust_copy.start()
    near = far - 2
    parts = ((0, far, 0), (1, near, far))

    def state_row(part, row):
        return row_at(view_ref, (part * rows + row) // SUBLANES, row % SUBLANES)

    def edges(low_ref, high_ref):
        for part, width, at in parts:
            for i in range(width):
                low_ref[at + i] = state_row(part, i)
                high_ref[at + i] = state_row(part, rows - width + i)

    for part, width, at in parts:
        copies[part].wait()
        for row in range(width, rows - width):
            mid_ref[part * (rows - 2 * far) + row - width] = state_row(part, row)

    @pl.when(odd_ref[0] == 0)
    def _():
        edges(first_ref, second_ref)

    @pl.when(odd_ref[0] != 0)
    def _():
        edges(second_ref, first_ref)

    gust_copy.wait()
    first_ref[far + near] = gusts_of(gust_ref)


def field_kernel(
    across_ref, along_ref, kl_hbm, gust_hbm, rigid_hbm, mass_hbm, load_hbm, stiff_ref, pull_ref,
    push_ref, gust_out, kl_ref, gust_ref, rigid_ref, mass_ref, load_ref, sems
):
    copies = [
        pltpu.make_async_copy(source, target, sems.at[at])
        for at, (source, target) in enumerate(
            (
                (kl_hbm, kl_ref),
                (gust_hbm, gust_ref),
                (rigid_hbm, rigid_ref),
                (mass_hbm, mass_ref),
                (load_hbm, load_ref),
            )
        )
    ]
    for copy in copies:
        copy.start()
    for copy in copies[:2]:
        copy.wait()
    gust_out[...] = gusts_of(gust_ref)
    rows = stiff_ref.shape[0]
    mixed = []
    for order in range(KL):
        total = kl_ref[order, 0] * along_ref[0]
        for other in range(1, KL):
            total = total + kl_ref[order, other] * along_ref[other]
        mixed.append(total)

    def factor_rows(group, carry):
        for row in range(SUBLANES):
            at = group * SUBLANES + row
            field = across_ref[0, at] * mixed[0]
            for order in range(1, KL):
                field = field + across_ref[order, at] * mixed[order]
            stiff_ref[at] = jnp.exp(0.5 * jnp.tanh(field))
        return carry

    lax.fori_loop(0, rows // SUBLANES, factor_rows, 0)
    for copy in copies[2:]:
        copy.wait()

    def group_rows(group, carry):
        for row in range(SUBLANES):
            at = group * SUBLANES + row
            mass = row_at(mass_ref, group, row)
            stiff_ref[at] = row_at(rigid_ref, group, row) * stiff_ref[at]
            pull_ref[at] = (KICK * (1.0 + DECAY) * STIFF_SCALE) * mass
            push_ref[at] = KICK * (mass * row_at(load_ref, group, row))
        return carry

    lax.fori_loop(0, rows // SUBLANES, group_rows, 0)


def beside(row):
    lane = lax.broadcasted_iota(jnp.int32, (SUBLANES, LANES), 1)
    sub = lax.broadcasted_iota(jnp.int32, (SUBLANES, LANES), 0)
    last_lane = lane == LANES - 1
    first_lane = lane == 0
    ends = (last_lane & (sub == SUBLANES - 1)) | (first_lane & (sub == 0))
    within = jnp.where(ends, 0.0, row)
    below = jnp.where(last_lane, pltpu.roll(within, 1, 0), row)
    above = jnp.where(first_lane, pltpu.roll(within, SUBLANES - 1, 0), row)
    return pltpu.roll(below, 1, 1) + pltpu.roll(above, LANES - 1, 1)


def splat(value):
    return jnp.full((SUBLANES, LANES), value, jnp.float32)


def gust_row(gust_ref, step_index):
    stage, at = divmod(step_index, FINE)
    return jnp.broadcast_to(gust_ref[stage, at:at + 1, :], (SUBLANES, LANES))


HALF_PULL = 1.0 / (1.0 + DECAY)


def fill_coef(coef, gust_ref, slot):
    for index in range(2 * FINE + 1):
        if index == 0:
            terms = splat(DECAY * TIME_STEP), gust_row(gust_ref, 0), splat(HALF_PULL)
        elif index == 2 * FINE:
            terms = (
                splat(DECAY / TIME_STEP),
                gust_row(gust_ref, index - 1) / TIME_STEP,
                splat(HALF_PULL / TIME_STEP),
            )
        else:
            both = DECAY * gust_row(gust_ref, index - 1) + gust_row(gust_ref, index)
            terms = splat(DECAY * DECAY), both, splat(1.0)
        for at, term in enumerate(terms):
            coef[index, at] = term

    @pl.when(slot == 0)
    def _():
        coef[FINE, 0] = splat(DECAY / TIME_STEP)
        coef[FINE, 1] = gust_row(gust_ref, FINE - 1) / TIME_STEP
        coef[FINE, 2] = splat(HALF_PULL / TIME_STEP)


def advance_rows(sweep, starts, count, offset, pos, vel, coef, stiff_ref, pull_ref, push_ref):
    here = [[pos[sweep, start - 2 + i] for i in range(count + 4)] for start in starts]
    sides = [[beside(rows[i]) for i in range(1, count + 3)] for rows in here]
    weighted = [
        [
            stiff_ref[start - 1 + i - offset]
            * (rows[i] + rows[i + 2] + side[i] - 4.0 * rows[i + 1])
            for i in range(count + 2)
        ]
        for start, rows, side in zip(starts, here, sides)
    ]
    weighted_sides = [[beside(row) for row in rows[1:-1]] for rows in weighted]
    alpha, push_by, pull_by = (coef[sweep, i] for i in range(3))
    moved = []
    for start, rows, heavy, side in zip(starts, here, weighted, weighted_sides):
        for i in range(count):
            row = start + i
            bent = heavy[i] + heavy[i + 2] + side[i] - 4.0 * heavy[i + 1]
            shift = (
                alpha * vel[sweep, row]
                + push_by * push_ref[row - offset]
                - pull_by * (pull_ref[row - offset] * bent)
            )
            moved.append((row, rows[i + 2] + shift, shift))
    return moved


def keep_rows(sweep, moved, pos, vel):
    for row, position, shift in moved:
        pos[sweep + 1, row] = position
        vel[sweep + 1, row] = shift


def inner_kernel(
    slot_ref, edge_ref, mid_ref, stiff_ref, pull_ref, push_ref, gust_ref, pos, vel, coef,
    *, rows, far
):
    near = far - 2
    side = far + near
    top = far + 2
    slot = slot_ref[0]
    fill_coef(coef, gust_ref, slot)
    inside = rows - 2 * far
    for plane_ref, width, at, first in ((pos, far, 0, 0), (vel, near, far, inside)):
        for i in range(width):
            plane_ref[0, top + i] = edge_ref[at + i]
            plane_ref[0, top + rows - width + i] = edge_ref[side + at + i]
        for i in range(rows - 2 * width):
            plane_ref[0, top + width + i] = mid_ref[first + i]

    def sweep_with(count):
        def sweep_all(sweep, carry):
            start = top + (rows - count) // 2
            moved = advance_rows(
                sweep, (start,), count, top, pos, vel, coef, stiff_ref, pull_ref, push_ref
            )
            keep_rows(sweep, moved, pos, vel)
            return carry

        return sweep_all

    early = 4
    sweeps = jnp.where(slot == 0, FINE + 1, 2 * FINE + 1)
    lax.fori_loop(0, early, sweep_with(rows - 4), 0)
    lax.fori_loop(early, sweeps, sweep_with(rows - 4 - 4 * early), 0)


def outer_kernel(
    slot_ref, odd_ref, inner_halo, outer_halo, stiff_ref, pull_ref, push_ref, gust_ref, pos_in,
    vel_in, coef, pos, vel, out_ref, *, rows, far
):
    near = far - 2
    top = far + 2
    slot = slot_ref[0]
    sweeps = jnp.where(slot == 0, FINE + 1, 2 * FINE + 1)

    def fill_halo(low, high):
        for i in range(far):
            pos[0, top - far + i] = low[i]
            pos[0, top + rows + i] = high[i]
        for i in range(near):
            vel[0, top - near + i] = low[far + i]
            vel[0, top + rows + i] = high[far + i]

    @pl.when(odd_ref[0] == 0)
    def _():
        fill_halo(outer_halo, inner_halo)

    @pl.when(odd_ref[0] != 0)
    def _():
        fill_halo(inner_halo, outer_halo)

    def sweep_all(sweep, carry):
        starts = (top - near + 2 * sweep, top + rows - 2 - 2 * sweep)
        moved = advance_rows(
            sweep, starts, far, 0, pos, vel, coef, stiff_ref, pull_ref, push_ref
        )
        keep_rows(sweep, moved, pos, vel)
        return carry

    lax.fori_loop(0, sweeps, sweep_all, 0)

    begin = slot * FINE
    own = slot == 0
    by_start = splat(jnp.where(own, TIME_STEP, DECAY * HALF_PULL))
    by_next = splat(jnp.where(own, 0.0, HALF_PULL))
    gust_step = gust_row(gust_ref, FINE - 1) - gust_row(gust_ref, FINE)
    by_push = jnp.where(own, 0.0, HALF_PULL) * gust_step

    def finish(group, carry):
        first = pl.multiple_of(group * SUBLANES * SUBLANES, SUBLANES * SUBLANES)
        for j in range(SUBLANES):
            row = group * SUBLANES + j + top
            following = vel[begin + 1, row]
            scaled = by_start * vel[begin, row] + by_next * following + by_push * push_ref[row]
            force = following - DECAY * scaled
            coarse_vel = (COARSE_DECAY / TIME_STEP) * scaled + (COARSE_SPAN / KICK) * force
            coarse_pos = pos[begin, row] + COARSE_SPAN * coarse_vel
            delta_pos = pos[sweeps - 1, row] - coarse_pos
            delta_vel = vel[sweeps, row] - coarse_vel
            at = first + j
            out_ref[pl.ds(at, SUBLANES, stride=SUBLANES), :] = coarse_pos + delta_pos
            out_ref[pl.ds(at + rows * SUBLANES, SUBLANES, stride=SUBLANES), :] = (
                coarse_vel + delta_vel
            )
        return carry

    lax.fori_loop(0, rows // SUBLANES, finish, 0)


def swap_pairs(count, first):
    pairs = [(i, i + 1) for i in range(first, count - 1, 2)]
    return pairs + [(target, source) for source, target in pairs]


def sent(block, pairs, within=None):
    if within is not None:
        base = within * lax.axis_size("space")
        pairs = [(base + source, base + target) for source, target in pairs]
    axes = "space" if within is None else ("tm", "space")
    return lax.ppermute(block, axes, pairs)


def in_vmem(count):
    return [pl.BlockSpec(memory_space=pltpu.VMEM)] * count


def in_smem(count):
    return [pl.BlockSpec(memory_space=pltpu.SMEM)] * count


def in_hbm(array):
    return pltpu.with_memory_space_constraint(array, pltpu.HBM)


def plane(count):
    return jax.ShapeDtypeStruct((count, SUBLANES, LANES), jnp.float32)


def field_call(across, along, kl_coeff, gust_history, rigidity, inv_mass, gust_load):
    rows = rigidity.shape[0] // SUBLANES
    return pl.pallas_call(
        field_kernel,
        out_shape=(plane(rows),) * 3 + (jax.ShapeDtypeStruct((SUBLANES, LANES), jnp.float32),),
        in_specs=in_smem(1) + in_vmem(1) + [pl.BlockSpec(memory_space=pltpu.HBM)] * 5,
        out_specs=tuple(in_vmem(4)),
        scratch_shapes=[
            pltpu.SMEM((KL, KL), jnp.float32),
            pltpu.SMEM((FINE,), jnp.float32),
        ]
        + [pltpu.VMEM(rigidity.shape, jnp.float32)] * 3
        + [pltpu.SemaphoreType.DMA((5,))],
        compiler_params=pltpu.CompilerParams(vmem_limit_bytes=16 * 2**20),
        name="field",
    )(
        across,
        along,
        in_hbm(kl_coeff),
        in_hbm(gust_history),
        in_hbm(rigidity),
        in_hbm(inv_mass),
        in_hbm(gust_load),
    )


def state_planes(rows, far):
    shape = (2 * FINE + 2, rows + 2 * far + 4, SUBLANES, LANES)
    return jax.ShapeDtypeStruct(shape, jnp.float32)


def coef_table():
    return jax.ShapeDtypeStruct((2 * FINE + 1, 3, SUBLANES, LANES), jnp.float32)


def inner_call(slot, edge, mid, stiff, pull, push, gusts, rows, far):
    return pl.pallas_call(
        functools.partial(inner_kernel, rows=rows, far=far),
        out_shape=(state_planes(rows, far),) * 2 + (coef_table(),),
        in_specs=in_smem(1) + in_vmem(6),
        out_specs=tuple(in_vmem(3)),
        compiler_params=pltpu.CompilerParams(vmem_limit_bytes=24 * 2**20),
        name="inner",
    )(slot, edge, mid, stiff, pull, push, gusts)


def outer_call(slot, odd, inner, outer, stiff, pull, push, gusts, pos, vel, coef, rows, far):
    planes = state_planes(rows, far)
    out = jax.ShapeDtypeStruct((2 * rows * SUBLANES, LANES), jnp.float32)
    return pl.pallas_call(
        functools.partial(outer_kernel, rows=rows, far=far),
        out_shape=(planes, planes, out),
        in_specs=in_smem(2) + in_vmem(9),
        out_specs=tuple(in_vmem(3)),
        input_output_aliases={8: 0, 9: 1},
        compiler_params=pltpu.CompilerParams(vmem_limit_bytes=24 * 2**20),
        name="outer",
    )(slot, odd, inner, outer, stiff, pull, push, gusts, pos, vel, coef)[2]


def two_slice_device(start_state, rigidity, inv_mass, gust_load, kl_coeff, gust_history):
    rows, cols = rigidity.shape
    far = 2 * (2 * FINE + 1)
    near = far - 2
    side = far + near
    time_slot = lax.axis_index("tm")
    space_slot = lax.axis_index("space")
    space_count = lax.axis_size("space")
    odd = space_slot % 2 == 1
    small = pltpu.CompilerParams(vmem_limit_bytes=16 * 2**20)

    slot = time_slot.reshape(1)
    parity = odd.astype(jnp.int32).reshape(1)
    first_own, second_own, mid_own = pl.pallas_call(
        functools.partial(pack_kernel, rows=rows, far=far),
        out_shape=(plane(side + 1), plane(side), plane(2 * rows - 2 * side)),
        in_specs=in_smem(2) + [pl.BlockSpec(memory_space=pltpu.HBM)] * 2,
        out_specs=tuple(in_vmem(3)),
        scratch_shapes=[
            pltpu.VMEM((2 * rows * SUBLANES, LANES), jnp.float32),
            pltpu.SMEM((FINE,), jnp.float32),
            pltpu.SemaphoreType.DMA((3,)),
        ],
        compiler_params=small,
        name="pack",
    )(slot, parity, in_hbm(gust_history), in_hbm(tile_view(start_state)))
    first_in = passed_along(first_own, "tm", 1)
    few = 2 * (FINE + 1)
    away = far - few
    early_rows = jnp.where(
        odd,
        jnp.concatenate([first_own[away:far], first_own[far + away:side]]),
        jnp.concatenate([first_own[:few], first_own[far:side - away]]),
    )
    early = sent(early_rows, swap_pairs(space_count, 1), 0)
    second_in = passed_along(second_own, "tm", 1)
    mid_in = passed_along(mid_own, "tm", 1)
    first_own, rigidity, inv_mass, gust_load = lax.optimization_barrier(
        (first_own, rigidity, inv_mass, gust_load)
    )

    across = mode_table(space_slot * rows + jnp.arange(rows), rows * lax.axis_size("space"))
    along = mode_table(jnp.arange(cols), cols).reshape(KL, SUBLANES, LANES)
    stiff, pull, push, own_gusts = field_call(
        across,
        along,
        kl_coeff,
        gust_history,
        tile_view(rigidity),
        tile_view(inv_mass),
        tile_view(gust_load),
    )
    wide = far - 1
    still_low = jnp.concatenate([stiff[:wide], pull[:near], push[:near]])
    still_high = jnp.concatenate(
        [stiff[rows - wide:], pull[rows - near:], push[rows - near:]]
    )
    still_outer = sent(jnp.where(odd, still_high, still_low), swap_pairs(space_count, 1))
    still_inner = sent(jnp.where(odd, still_low, still_high), swap_pairs(space_count, 0))

    own = time_slot == 0
    first_edge = jnp.where(own, first_own, first_in)
    mid = jnp.where(own, mid_own, mid_in)
    outer_late = sent(first_in, swap_pairs(space_count, 1), 1)
    second_edge = jnp.where(own, second_own, second_in)
    edge = jnp.concatenate(
        [
            jnp.where(odd, second_edge, first_edge[:side]),
            jnp.where(odd, first_edge[:side], second_edge),
        ]
    )
    inner = sent(second_edge, swap_pairs(space_count, 0))
    gusts = jnp.stack([first_edge[side], own_gusts])
    pos, vel, coef = inner_call(slot, edge, mid, stiff, pull, push, gusts, rows, far)

    blank = jnp.zeros((away, SUBLANES, LANES), jnp.float32)
    of_even = jnp.concatenate([early[:few], blank, early[few:], blank])
    of_odd = jnp.concatenate([blank, early[:few], blank, early[few:]])
    outer = jnp.where(own, jnp.where(odd, of_even, of_odd), outer_late[:side])
    low = jnp.where(odd, still_inner, still_outer)
    high = jnp.where(odd, still_outer, still_inner)

    def spread(low_rows, own_rows, high_rows):
        margin = far + 2 - low_rows.shape[0]
        block = jnp.concatenate([low_rows, own_rows, high_rows])
        return jnp.pad(block, ((margin, margin), (0, 0), (0, 0)))

    stiff = spread(low[:wide], stiff, high[:wide])
    pull = spread(low[wide:wide + near], pull, high[wide:wide + near])
    push = spread(low[wide + near:], push, high[wide + near:])
    out = outer_call(
        slot, parity, inner, outer, stiff, pull, push, gusts, pos, vel, coef, rows, far
    )
    return from_tile_view(out, start_state.shape)


def layered_device(*args):
    return two_slice_device(*args)


def chosen_device(start_state, rigidity, inv_mass, gust_load, kl_coeff, gust_history):
    rows, cols = rigidity.shape
    fits = cols == SUBLANES * LANES and rows % SUBLANES == 0 and rows >= UNROLL + 4
    two_slices = lax.axis_size("tm") == 2 and ITERS == 2 and start_state.shape[0] == 1
    device = layered_device if fits and two_slices else per_device
    return device(start_state, rigidity, inv_mass, gust_load, kl_coeff, gust_history)


def solution(mesh):
    in_specs = (
        P("tm", None, "space", None),
        P("space", None),
        P("space", None),
        P("space", None),
        P(),
        P("tm"),
    )
    out_specs = P("tm", None, "space", None)
    return jax.shard_map(
        chosen_device, mesh=mesh, in_specs=in_specs, out_specs=out_specs, check_vma=False
    )
```
